128 devices in a mesh: row: 8 (over y, core), col: 16 (over z, x).
Axes of the slice: x: 4, y: 4, z: 4, core: 2. Of those that a mesh axis runs over, the one named last changes fastest.
Arguments:
- dealing: int32 [8, 16], P('row'), may hold values from 0 to 15, each once within a row
- residual: bfloat16 [8192, 3072], P('row', 'col'), may hold values from -6 to 6
- queries: bfloat16 [8192, 3072], P('row', 'col'), may hold values from -6 to 6
- draft_keys: bfloat16 [8192, 3072], P('row', 'col'), may hold values from -6 to 6
- draft_values: bfloat16 [8192, 3072], P('row', 'col'), may hold values from -6 to 6
- cache_keys: bfloat16 [128, 1536, 3072], P(('row', 'col')), may hold values from -6 to 6
- cache_values: bfloat16 [128, 1536, 3072], P(('row', 'col')), may hold values from -6 to 6
- cache_lengths: int32 [128], P(('row', 'col')), may hold values from 97 to 1536, as said below
- parents: int32 [128, 64], P(('row', 'col')), may hold values from -1 to 62, as said below
- draft_counts: int32 [128], P(('row', 'col')), may hold values from 32 to 64, as said below
- accepted: int32 [128, 8], P(('row', 'col')), may hold values from -1 to 28, as said below
- out_weight: bfloat16 [3072, 3072], P('row', 'col'), may hold values from -0.109375 to 0.109375
- norm_gain: bfloat16 [3072], P('col'), may hold values from 0.099609375 to 1.8984375
- gate_weight: bfloat16 [3072, 8192], P('row', 'col'), may hold values from -0.109375 to 0.109375
- up_weight: bfloat16 [3072, 8192], P('row', 'col'), may hold values from -0.109375 to 0.109375
- down_weight: bfloat16 [8192, 3072], P('col', 'row'), may hold values from -0.09375 to 0.09375
Outputs:
- layer_out: bfloat16 [8192, 3072], P('row', 'col')
- new_keys: bfloat16 [128, 8, 3072], P(('row', 'col'))
- new_values: bfloat16 [128, 8, 3072], P(('row', 'col'))
The draws below stay inside these ranges and needn't reach their ends.
Inputs may be any that keep to these rules, and one draw needn't show every extreme that they name: Each row of dealing names every index along col once. `cache_lengths`: the largest is 1536 in every draw. parents[s, 0] = -1, and for i >= 1, i - 4 <= parents[s, i] < i. `draft_counts`: the largest is 64 in every draw. `accepted`: each row lists draft tokens from the root 0 downward, each the child under parents of the one before and below the slot's draft count, then -1; some row fills all 8 entries, and the largest entry is 28 in every draw.
All inputs are finite; a program needn't handle non-finite values.
Results may differ from the reference program's by a relative error of at most 0.017.
Values may be sent and summed in bfloat16 or wider, within the bound.
A program may use at most 128 MiB of HBM per device.

```python
import math
import jax
import jax.numpy as jnp
from jax import lax

D = 3072
HEADS = 32
HEAD_DIM = 96
FF = 8192
DRAFT = 64
PATH = 8
CACHE = 1536
REQUESTS = 128
TOKENS = 8192
N_ROW = 8
N_COL = 16


def longest_request(key):
    return jax.random.randint(jax.random.fold_in(key, 104), (), 0, REQUESTS)


def tree_parents(key):
    backward = jax.random.randint(jax.random.fold_in(key, 101), (REQUESTS, DRAFT), 0, 4)
    forced = (jnp.arange(REQUESTS) == longest_request(key))[:, None]
    backward = jnp.where(forced, 3, backward)
    token_index = jnp.arange(DRAFT, dtype=jnp.int32)[None, :]
    linked = jnp.maximum(token_index - 1 - backward, 0)
    return jnp.where(token_index == 0, -1, linked).astype(jnp.int32)


def token_counts(key):
    counts = jax.random.randint(jax.random.fold_in(key, 102), (REQUESTS,), DRAFT // 2, DRAFT + 1)
    longest = longest_request(key)
    return jnp.where(jnp.arange(REQUESTS) == longest, DRAFT, counts).astype(jnp.int32)


def draw_parents(key, part):
    return tree_parents(key)


def draw_draft_counts(key, part):
    return token_counts(key)


def draw_accepted(key, part):
    parent_table = tree_parents(key)
    counts = token_counts(key)
    chosen_node = jax.random.randint(jax.random.fold_in(key, 103), (REQUESTS,), 0, counts)
    chosen_node = jnp.where(counts == DRAFT, DRAFT - 1, chosen_node)
    chosen_node = jnp.where(jnp.arange(REQUESTS) == longest_request(key), DRAFT - 4, chosen_node)

    def climb(parent_row, start_node):

        def upward(current, unused):
            following = jnp.where(current > 0, parent_row[jnp.maximum(current, 0)], -1)
            return (following, current)
        last_node, ancestor_chain = lax.scan(upward, start_node, None, length=DRAFT)
        tree_depth = jnp.sum(ancestor_chain >= 0) - 1
        path_slot = jnp.arange(PATH, dtype=jnp.int32)
        source = jnp.clip(tree_depth - path_slot, 0, DRAFT - 1)
        return jnp.where(path_slot <= jnp.minimum(tree_depth, PATH - 1), ancestor_chain[source], -1)
    return jax.vmap(climb)(parent_table, chosen_node).astype(jnp.int32)


def draw_cache_lengths(key, part):
    key_one, key_two, key_three = jax.random.split(key, 3)
    halvings = jax.random.randint(key_one, (REQUESTS,), 0, 4)
    base_length = jnp.right_shift(jnp.full((REQUESTS,), CACHE, jnp.int32), halvings)
    trimmed = jax.random.randint(key_two, (REQUESTS,), 0, base_length // 2)
    lengths = base_length - trimmed
    longest = jax.random.randint(key_three, (), 0, REQUESTS)
    return jnp.where(jnp.arange(REQUESTS) == longest, CACHE, lengths).astype(jnp.int32)


def drawn_pair(key):
    key_one, key_two = jax.random.split(key, 2)
    query_draw = jnp.clip(jax.random.normal(key_one, (TOKENS, D), jnp.float32), -6.0, 6.0)
    key_draw = jnp.clip(jax.random.normal(key_two, (TOKENS, D), jnp.float32), -6.0, 6.0)
    return (query_draw, key_draw)


def draw_queries(key, part):
    return drawn_pair(jax.random.fold_in(key, 201))[0].astype(jnp.bfloat16)


def draw_draft_keys(key, part):
    return drawn_pair(jax.random.fold_in(key, 201))[1].astype(jnp.bfloat16)


def spiked(values, stream_key, source, target, parts, factor):
    owner, partner = [(jnp.arange(values.shape[axis_at]) // (values.shape[axis_at] // parts)).reshape([-1 if axis == axis_at else 1 for axis in range(values.ndim)]) for axis_at in (source, target)]
    chosen = jax.random.permutation(stream_key, parts)[partner]
    strong = (owner == chosen) | (owner == (partner + parts // 2) % parts)
    return jnp.where(strong, factor * values, values)


def block_scale(rng, shape, shards, least, top_value):
    gain = 1.0
    for dim, parts in shards:
        heights = jax.random.uniform(jax.random.fold_in(jax.random.fold_in(rng, 6), dim), (parts,), jnp.float32, least / len(shards), top_value / len(shards))
        gain = gain * jnp.repeat(jnp.exp(heights), shape[dim] // parts).reshape((-1,) + (1,) * (len(shape) - 1 - dim))
    return gain


def normal_values(rng, dims, deviation, most, cuts=(), kind=jnp.bfloat16):
    values = deviation * jax.random.normal(rng, dims, jnp.float32)
    if cuts:
        values = values * block_scale(rng, dims, cuts, -0.22, 0.18)
    return jnp.clip(values, -most, most).astype(kind)


def gaussian_with(stream_key, dims, spread, reach, cuts, heavy, kind=jnp.bfloat16):
    values = spread * jax.random.normal(stream_key, dims, jnp.float32)
    if cuts:
        values = values * block_scale(stream_key, dims, cuts, -0.22, 0.18)
    return jnp.clip(spiked(values, jax.random.fold_in(stream_key, 3), *heavy), -reach, reach).astype(kind)


def setup_inputs(seed: int = 0) -> dict:
    key_of = jax.random.split(jax.random.key(seed), 17)
    return {
        "dealing": jax.vmap(lambda own: jax.random.permutation(own, N_COL))(jax.random.split(key_of[0], N_ROW)).reshape((N_ROW, N_COL)).astype(jnp.int32),
        "residual": normal_values(key_of[1], (TOKENS, D), 1.0, 6.0, ((0, 8), (1, 16))),
        "queries": draw_queries(jax.random.fold_in(key_of[16], 71), 0),
        "draft_keys": draw_draft_keys(jax.random.fold_in(key_of[16], 71), 0),
        "draft_values": normal_values(key_of[4], (TOKENS, D), 1.0, 6.0, ((0, 8), (1, 16))),
        "cache_keys": normal_values(key_of[5], (REQUESTS, CACHE, D), 1.0, 6.0, ((0, 128),)),
        "cache_values": normal_values(key_of[6], (REQUESTS, CACHE, D), 1.0, 6.0, ((0, 128),)),
        "cache_lengths": draw_cache_lengths(jax.random.fold_in(key_of[16], 71), 0),
        "parents": draw_parents(jax.random.fold_in(key_of[16], 71), 0),
        "draft_counts": draw_draft_counts(jax.random.fold_in(key_of[16], 71), 0),
        "accepted": draw_accepted(jax.random.fold_in(key_of[16], 71), 0),
        "out_weight": normal_values(key_of[11], (D, D), D ** -0.5, 0.109375, ((0, 8), (1, 16))),
        "norm_gain": jnp.clip(1.0 + 0.18 * jax.random.normal(key_of[12], (D,), jnp.float32), 0.099609375, 1.8984375).astype(jnp.bfloat16),
        "gate_weight": normal_values(key_of[13], (D, FF), D ** -0.5, 0.109375, ((0, 8), (1, 16))),
        "up_weight": normal_values(key_of[14], (D, FF), D ** -0.5, 0.109375, ((0, 8), (1, 16))),
        "down_weight": gaussian_with(key_of[15], (FF, D), FF ** -0.5, 0.09375, ((0, 16), (1, 8)), (0, 1, 16, 2.0)),
    }


def ancestry(parent_row):
    count_all = parent_row.shape[0]
    token_index = jnp.arange(count_all, dtype=jnp.int32)
    linked = jnp.logical_or(parent_row[:, None] == token_index[None, :], token_index[:, None] == token_index[None, :])
    ancestors = linked.astype(jnp.float32)
    for sweep in range(max(1, (count_all - 1).bit_length())):
        ancestors = jnp.minimum(jnp.dot(ancestors, ancestors, precision=lax.Precision.HIGHEST), 1.0)
    return ancestors

def rotate(value_rows, position):
    row_count = value_rows.shape[0]
    half_dim = HEAD_DIM // 2
    shaped = value_rows.astype(jnp.float32).reshape(row_count, HEADS, HEAD_DIM)
    frequency = jnp.power(10000.0, -jnp.arange(half_dim, dtype=jnp.float32) * (2.0 / HEAD_DIM))
    angles = position[:, None] * frequency[None, :]
    cosine = jnp.cos(angles)[:, None, :]
    sine_part = jnp.sin(angles)[:, None, :]
    front_half = shaped[..., :half_dim]
    back_half = shaped[..., half_dim:]
    turned = jnp.concatenate([front_half * cosine - back_half * sine_part, back_half * cosine + front_half * sine_part], axis=-1)
    return turned.reshape(row_count, HEADS * HEAD_DIM).astype(jnp.bfloat16)

def verify_slot(query_rows, key_rows, value_rows, cache_k, cache_v, length, parent_row, live_count, path_row):
    ancestors = ancestry(parent_row)
    tree_depth = lax.optimization_barrier(jnp.sum(ancestors, axis=1)) - 1.0
    position = length.astype(jnp.float32) + tree_depth
    q_rot = rotate(query_rows, position)
    k_rot = rotate(key_rows, position)
    score_scale = 1.0 / math.sqrt(HEAD_DIM)
    q_heads = q_rot.astype(jnp.float32).reshape(DRAFT, HEADS, HEAD_DIM)
    all_keys = jnp.concatenate([cache_k, k_rot], axis=0).astype(jnp.float32).reshape(CACHE + DRAFT, HEADS, HEAD_DIM)
    all_values = jnp.concatenate([cache_v, value_rows], axis=0).astype(jnp.float32).reshape(CACHE + DRAFT, HEADS, HEAD_DIM)
    scores = jnp.einsum('qhd,khd->hqk', q_heads, all_keys) * score_scale
    token_index = jnp.arange(DRAFT, dtype=jnp.int32)
    cache_live = jnp.arange(CACHE, dtype=jnp.int32) < length
    draft_live = jnp.logical_and(ancestors > 0.5, token_index[None, :] < live_count)
    allowed = jnp.concatenate([jnp.broadcast_to(cache_live[None, :], (DRAFT, CACHE)), draft_live], axis=1)
    scores = jnp.where(allowed[None], scores, -jnp.inf)
    row_max = lax.optimization_barrier(jnp.max(scores, axis=2, keepdims=True))
    weights = jnp.exp(scores - row_max)
    totals = lax.optimization_barrier(jnp.sum(weights, axis=2))
    rounded = lax.optimization_barrier(weights.astype(jnp.bfloat16)).astype(jnp.float32)
    mixed_rows = jnp.einsum('hqk,khd->qhd', rounded, all_values)
    attended = (mixed_rows / totals.T[:, :, None]).reshape(DRAFT, HEADS * HEAD_DIM).astype(jnp.bfloat16)
    selector = (path_row[:, None] == token_index[None, :]).astype(jnp.float32)
    new_keys = jnp.dot(selector, k_rot.astype(jnp.float32), precision=lax.Precision.HIGHEST).astype(jnp.bfloat16)
    new_values = jnp.dot(selector, value_rows.astype(jnp.float32), precision=lax.Precision.HIGHEST).astype(jnp.bfloat16)
    return (attended, new_keys, new_values)

def reference(dealing, residual, queries, draft_keys, draft_values, cache_keys, cache_values, cache_lengths, parents, draft_counts, accepted, out_weight, norm_gain, gate_weight, up_weight, down_weight):
    owner = (jnp.arange(N_ROW, dtype=jnp.int32)[:, None] * N_COL + dealing).reshape(-1)

    def by_slot(flat_rows):
        return jnp.take(flat_rows.reshape(REQUESTS, DRAFT, D), owner, axis=0)
    items = (by_slot(queries), by_slot(draft_keys), by_slot(draft_values), cache_keys, cache_values, cache_lengths, parents, draft_counts, accepted)
    attended, new_keys, new_values = lax.map(lambda item_set: verify_slot(*item_set), items)
    inverse = jnp.argsort(owner)
    attended = jnp.take(attended, inverse, axis=0).reshape(TOKENS, D)
    stream_full = residual.astype(jnp.float32) + jnp.dot(attended, out_weight, preferred_element_type=jnp.float32)
    stream_wide = lax.optimization_barrier(stream_full.astype(jnp.bfloat16)).astype(jnp.float32)
    factor = lax.rsqrt(lax.optimization_barrier(jnp.mean(stream_wide * stream_wide, axis=1, keepdims=True)) + 1e-05)
    normed = (stream_wide * factor * norm_gain.astype(jnp.float32)[None, :]).astype(jnp.bfloat16)
    gate_sum = jnp.dot(normed, gate_weight, preferred_element_type=jnp.float32)
    up_sum = jnp.dot(normed, up_weight, preferred_element_type=jnp.float32)
    hidden = (jax.nn.silu(gate_sum) * up_sum).astype(jnp.bfloat16)
    block_width = FF // N_COL

    def add_block(running, block_number):
        hidden_part = lax.dynamic_slice_in_dim(hidden, block_number * block_width, block_width, 1)
        weight_part = lax.dynamic_slice_in_dim(down_weight, block_number * block_width, block_width, 0)
        partial_value = jnp.dot(hidden_part, weight_part, preferred_element_type=jnp.float32).astype(jnp.bfloat16)
        return (running + partial_value.astype(jnp.float32), None)
    mlp_sum, unused = lax.scan(add_block, jnp.zeros((TOKENS, D), jnp.float32), jnp.arange(N_COL, dtype=jnp.int32))
    layer_out = (stream_wide + mlp_sum).astype(jnp.bfloat16)
    return (layer_out, new_keys, new_values)
```

```python
import math

import jax
import jax.numpy as jnp
from jax import lax
from jax.experimental import pallas as pl
from jax.experimental.pallas import tpu as pltpu
from jax.sharding import PartitionSpec as P

D = 3072
HEADS = 32
HEAD_DIM = 96
MESH = pl.DeviceIdType.MESH


def ancestry(parent_row):
    count_all = parent_row.shape[0]
    token_index = jnp.arange(count_all, dtype=jnp.int32)
    linked = jnp.logical_or(
        parent_row[:, None] == token_index[None, :], token_index[:, None] == token_index[None, :]
    )
    ancestors = linked.astype(jnp.float32)
    for sweep in range(max(1, (count_all - 1).bit_length())):
        ancestors = jnp.minimum(jnp.dot(ancestors, ancestors, precision=lax.Precision.HIGHEST), 1.0)
    return ancestors


def rotate(value_rows, position):
    row_count = value_rows.shape[0]
    half_dim = HEAD_DIM // 2
    shaped = value_rows.astype(jnp.float32).reshape(row_count, HEADS, HEAD_DIM)
    frequency = jnp.power(10000.0, -jnp.arange(half_dim, dtype=jnp.float32) * (2.0 / HEAD_DIM))
    angles = position[:, None] * frequency[None, :]
    cosine = jnp.cos(angles)[:, None, :]
    sine_part = jnp.sin(angles)[:, None, :]
    front_half = shaped[..., :half_dim]
    back_half = shaped[..., half_dim:]
    turned = jnp.concatenate(
        [front_half * cosine - back_half * sine_part, back_half * cosine + front_half * sine_part],
        axis=-1,
    )
    return turned.reshape(row_count, HEADS * HEAD_DIM).astype(jnp.bfloat16)


def fold_block(state_now, q_heads, key_block, value_block, allowed):
    running_max, row_totals, accumulator = state_now
    score_scale = 1.0 / math.sqrt(HEAD_DIM)
    key_heads = key_block.reshape(key_block.shape[0], HEADS, HEAD_DIM)
    value_heads = value_block.reshape(value_block.shape[0], HEADS, HEAD_DIM)
    scores = (
        jnp.einsum("qhd,khd->hqk", q_heads, key_heads, preferred_element_type=jnp.float32)
        * score_scale
    )
    scores = jnp.where(allowed[None], scores, -jnp.inf)
    new_max = jnp.maximum(running_max, jnp.max(scores, axis=2))
    rescale = jnp.exp(running_max - new_max)
    weights = jnp.exp(scores - new_max[:, :, None])
    row_totals = row_totals * rescale + jnp.sum(weights, axis=2)
    mixed_rows = jnp.einsum(
        "hqk,khd->qhd",
        weights.astype(jnp.bfloat16),
        value_heads,
        preferred_element_type=jnp.float32,
    )
    accumulator = accumulator * rescale.T[:, :, None] + mixed_rows
    return (new_max, row_totals, accumulator)


def verify_slot(
    query_rows, key_rows, value_rows, cache_k, cache_v, length, parent_row, live_count, path_row
):
    draft_rows = query_rows.shape[0]
    width = query_rows.shape[1]
    ancestors = ancestry(parent_row)
    tree_depth = jnp.sum(ancestors, axis=1) - 1.0
    position = length.astype(jnp.float32) + tree_depth
    q_rot = rotate(query_rows, position)
    k_rot = rotate(key_rows, position)
    q_heads = q_rot.reshape(draft_rows, HEADS, HEAD_DIM)
    cache_rows = cache_k.shape[0]
    block_rows = min(512, cache_rows)

    def cache_step(block_step, state_now):
        block_start = block_step * block_rows
        key_block = lax.dynamic_slice_in_dim(cache_k, block_start, block_rows, 0)
        value_block = lax.dynamic_slice_in_dim(cache_v, block_start, block_rows, 0)
        live_keys = block_start + jnp.arange(block_rows, dtype=jnp.int32) < length
        allowed = jnp.broadcast_to(live_keys[None, :], (draft_rows, block_rows))
        return fold_block(state_now, q_heads, key_block, value_block, allowed)

    initial = (
        jnp.full((HEADS, draft_rows), -jnp.inf, jnp.float32),
        jnp.zeros((HEADS, draft_rows), jnp.float32),
        jnp.zeros((draft_rows, HEADS, HEAD_DIM), jnp.float32),
    )
    block_total = cache_rows // block_rows
    state_now = lax.fori_loop(0, block_total, cache_step, initial)
    token_index = jnp.arange(draft_rows, dtype=jnp.int32)
    allowed = jnp.logical_and(ancestors > 0.5, token_index[None, :] < live_count)
    running_max, row_totals, accumulator = fold_block(
        state_now, q_heads, k_rot, value_rows, allowed
    )
    attended = (
        (accumulator / row_totals.T[:, :, None]).reshape(draft_rows, width).astype(jnp.bfloat16)
    )
    selector = (path_row[:, None] == token_index[None, :]).astype(jnp.bfloat16)
    new_keys = jnp.dot(selector, k_rot, preferred_element_type=jnp.float32).astype(jnp.bfloat16)
    new_values = jnp.dot(selector, value_rows, preferred_element_type=jnp.float32).astype(
        jnp.bfloat16
    )
    return (attended, new_keys, new_values)


def mlp_kernel(
    st_hbm, w_hbm, dn_hbm, gain_ref, out_ref,
    S, W, DN, acc, H, ss, T, R, Q, T2, R2,
    loc_sem, ag_send, ag_recv, rs_send, rs_recv, rt_send, rt_recv,
):
    me = lax.axis_index("col")
    z, x = me // 4, me % 4
    halves = (0, 1)
    a_own, b_own = (x, z), (z, x)

    def blk(h, a, b):
        return b * 4 + a if h == 0 else a * 4 + b

    def peer1(h, d):
        return blk(h, (a_own[h] + d + 4) % 4, b_own[h])

    def peer2(h, d):
        return blk(h, a_own[h], (b_own[h] + d + 4) % 4)

    stream_in = [
        pltpu.make_async_copy(st_hbm.at[:, pl.ds(512 * h, 512)], S.at[h, me], loc_sem.at[h])
        for h in halves
    ]
    w_in = pltpu.make_async_copy(w_hbm, W, loc_sem.at[2])
    dn_in = pltpu.make_async_copy(dn_hbm, DN, loc_sem.at[3])
    for c in stream_in:
        c.start()
    w_in.start()
    dn_in.start()

    barrier = pltpu.get_barrier_semaphore()
    for p in (peer1(0, 1), peer1(0, -1), peer1(1, 1), peer1(1, -1)):
        pl.semaphore_signal(barrier, inc=1, device_id={"col": p}, device_id_type=MESH)
    pl.semaphore_wait(barrier, 4)
    for c in stream_in:
        c.wait()

    sent = []

    def push(h, k, c, target, rows=None):
        ref = S.at[h, c] if rows is None else S.at[h, c, pl.ds(rows, 96)]
        cp = pltpu.make_async_remote_copy(
            src_ref=ref, dst_ref=ref, send_sem=ag_send.at[h, k], recv_sem=ag_recv.at[h, k],
            device_id={"col": target}, device_id_type=MESH,
        )
        cp.start()
        sent.append(cp)

    def arrived(h, k, c, rows=None):
        ref = S.at[h, c] if rows is None else S.at[h, c, pl.ds(rows, 96)]
        pltpu.make_async_remote_copy(
            src_ref=ref, dst_ref=ref, send_sem=ag_send.at[h, k], recv_sem=ag_recv.at[h, k],
            device_id={"col": me}, device_id_type=MESH,
        ).wait_recv()

    def at(h, da, db):
        return blk(h, (a_own[h] + da + 4) % 4, (b_own[h] + db + 4) % 4)

    offs = (0, -1, 1, 2)
    for h in halves:
        push(h, 0, me, peer1(h, 1))
        push(h, 1, me, peer1(h, -1))
    for h in halves:
        push(h, 4, me, peer2(h, 1))
        push(h, 5, me, peer2(h, -1))

    acc[...] = jnp.zeros_like(acc)
    ss[...] = jnp.zeros_like(ss)
    w_in.wait()

    @pl.loop(0, 8)
    def _(r):
        W[r] = W[r] * gain_ref[r]

    for h in halves:
        arrived(h, 0, at(h, -1, 0))
        push(h, 2, at(h, -1, 0), peer1(h, 1), 0)
        push(h, 8, at(h, -1, 0), peer2(h, 1))
        push(h, 9, at(h, -1, 0), peer2(h, -1))
        arrived(h, 1, at(h, 1, 0))
        push(h, 3, at(h, 1, 0), peer1(h, -1), 96)
        push(h, 12, at(h, 1, 0), peer2(h, 1))
        push(h, 13, at(h, 1, 0), peer2(h, -1))

    def second(j):
        for h in halves:
            base = 4 + 4 * j
            arrived(h, base, at(h, offs[j], -1))
            push(h, base + 2, at(h, offs[j], -1), peer2(h, 1), 0)
            arrived(h, base + 1, at(h, offs[j], 1))
            push(h, base + 3, at(h, offs[j], 1), peer2(h, -1), 96)

    def square(h, c):
        v = S[h, c].astype(jnp.float32)
        ss[h] += jnp.sum(v * v, axis=0, keepdims=True)

    def fold_a(zz):
        for i in range(4):
            square(0, zz * 4 + i)
        k0 = S[0, pl.ds(zz * 4, 2)].reshape(384, 512)
        k1 = S[0, pl.ds(zz * 4 + 2, 2)].reshape(384, 512)

        @pl.loop(0, 4)
        def _(m):
            rows = pl.ds(pl.multiple_of(m * 256, 256), 256)
            acc[0, rows] += jnp.dot(
                W[2 * zz, rows], k0, preferred_element_type=jnp.float32
            ) + jnp.dot(W[2 * zz + 1, rows], k1, preferred_element_type=jnp.float32)

    def fold_b(q):
        @pl.loop(0, 2)
        def _(g):
            for i in range(2):
                for e in range(2):
                    square(1, (2 * g + i) * 4 + 2 * q + e)
            k0 = S[1, pl.ds(8 * g + 2 * q, 2)].reshape(384, 512)
            k1 = S[1, pl.ds(8 * g + 4 + 2 * q, 2)].reshape(384, 512)

            @pl.loop(0, 4)
            def _(m):
                rows = pl.ds(pl.multiple_of(m * 256, 256), 256)
                acc[1, rows] += jnp.dot(
                    W[4 * g + q, rows], k0, preferred_element_type=jnp.float32
                ) + jnp.dot(W[4 * g + 2 + q, rows], k1, preferred_element_type=jnp.float32)

    second(0)
    for h in halves:
        arrived(h, 2, at(h, 2, 0), 0)
        arrived(h, 3, at(h, 2, 0), 96)
        push(h, 16, at(h, 2, 0), peer2(h, 1))
        push(h, 17, at(h, 2, 0), peer2(h, -1))
    fold_a(z)
    second(1)
    second(2)
    second(3)

    @pl.loop(0, 2)
    def _(i):
        fold_a((z + 3 + 2 * i) % 4)

    fold_b(x // 2)
    for h in halves:
        for j in range(4):
            arrived(h, 6 + 4 * j, at(h, offs[j], 2), 0)
            arrived(h, 7 + 4 * j, at(h, offs[j], 2), 96)
    fold_a((z + 2) % 4)
    fold_b(1 - x // 2)
    for cp in sent:
        cp.wait_send()

    for h in halves:
        factor = lax.rsqrt(ss[h] * (1.0 / D) + 1e-05)

        @pl.loop(0, 4)
        def _(m, h=h, factor=factor):
            rows = pl.ds(pl.multiple_of(m * 128, 128), 128)
            uprows = pl.ds(pl.multiple_of(512 + m * 128, 128), 128)
            g = acc[h, rows] * factor
            u = acc[h, uprows] * factor
            H[h, rows] = (g / (1.0 + jnp.exp(-g)) * u).astype(jnp.bfloat16)

    dn_in.wait()

    def part(h, c):
        rows = pl.ds(pl.multiple_of(c * 192, 192), 192)
        return jnp.dot(DN[rows], H[h], preferred_element_type=jnp.float32)

    sent = []

    def send1(h, kind, i):
        d = 1 if kind % 2 == 0 else -1
        cp = pltpu.make_async_remote_copy(
            src_ref=T.at[h, kind, i], dst_ref=R.at[h, kind, i],
            send_sem=rs_send.at[h, kind, i], recv_sem=rs_recv.at[h, kind, i],
            device_id={"col": peer1(h, d)}, device_id_type=MESH,
        )
        cp.start()
        sent.append(cp)

    def got1(h, kind, i):
        pltpu.make_async_remote_copy(
            src_ref=T.at[h, kind, i], dst_ref=R.at[h, kind, i],
            send_sem=rs_send.at[h, kind, i], recv_sem=rs_recv.at[h, kind, i],
            device_id={"col": me}, device_id_type=MESH,
        ).wait_recv()

    def dest(h, da, b):
        return blk(h, (a_own[h] + da + 4) % 4, b)

    for kind, da, b0 in ((0, 2, 0), (1, 2, 2), (4, 1, 2), (5, -1, 0)):
        for i in range(2):
            for h in halves:
                T[h, kind, i] = part(h, dest(h, da, b0 + i)).astype(jnp.bfloat16)
                send1(h, kind, i)
    for kind, da, b0 in ((2, 1, 0), (3, -1, 2)):
        for i in range(2):
            for h in halves:
                mine = part(h, dest(h, da, b0 + i))
                got1(h, kind - 2, i)
                T[h, kind, i] = (mine + R[h, kind - 2, i].astype(jnp.float32)).astype(jnp.bfloat16)
                send1(h, kind, i)
    for b in range(4):
        for h in halves:
            mine = part(h, dest(h, 0, b))
            s_kind, d_kind = (2, 5) if b < 2 else (3, 4)
            got1(h, s_kind, b % 2)
            got1(h, d_kind, b % 2)
            Q[h, b] = (
                mine
                + R[h, s_kind, b % 2].astype(jnp.float32)
                + R[h, d_kind, b % 2].astype(jnp.float32)
            ).astype(jnp.bfloat16)
    for h in halves:
        for i in range(2):
            pass

    def copy2(h, kind, src, target):
        return pltpu.make_async_remote_copy(
            src_ref=src, dst_ref=R2.at[h, kind],
            send_sem=rt_send.at[h, kind], recv_sem=rt_recv.at[h, kind],
            device_id={"col": target}, device_id_type=MESH,
        )

    def bmod(h, d):
        return (b_own[h] + d + 4) % 4

    for h in halves:
        for kind, d, row in ((0, 2, 0), (1, 2, 96), (4, 1, 96), (5, -1, 0)):
            cp = copy2(h, kind, Q.at[h, bmod(h, d), pl.ds(row, 96)], peer2(h, 1 if kind % 2 == 0 else -1))
            cp.start()
            sent.append(cp)
    for h in halves:
        for kind, d, row in ((2, 1, 0), (3, -1, 96)):
            copy2(h, kind - 2, T2.at[h, 0], me).wait_recv()
            T2[h, kind - 2] = (
                Q[h, bmod(h, d), pl.ds(row, 96)].astype(jnp.float32)
                + R2[h, kind - 2].astype(jnp.float32)
            ).astype(jnp.bfloat16)
            cp = copy2(h, kind, T2.at[h, kind - 2], peer2(h, 1 if kind == 2 else -1))
            cp.start()
            sent.append(cp)
    for h in halves:
        for row, s_kind, d_kind in ((0, 2, 5), (96, 3, 4)):
            copy2(h, s_kind, T2.at[h, 0], me).wait_recv()
            copy2(h, d_kind, T2.at[h, 0], me).wait_recv()
            out_ref[pl.ds(row, 96), pl.ds(512 * h, 512)] = (
                S[h, me, pl.ds(row, 96)].astype(jnp.float32)
                + Q[h, b_own[h], pl.ds(row, 96)].astype(jnp.float32)
                + R2[h, s_kind].astype(jnp.float32)
                + R2[h, d_kind].astype(jnp.float32)
            ).astype(jnp.bfloat16)
    for cp in sent:
        cp.wait_send()


def mlp_call(stream_t, weights, down_t, gain):
    anyspace = pl.BlockSpec(memory_space=pl.ANY)
    vmem = pl.BlockSpec(memory_space=pltpu.VMEM)
    bf, f32 = jnp.bfloat16, jnp.float32
    dma = pltpu.SemaphoreType.DMA
    return pl.pallas_call(
        mlp_kernel,
        out_shape=jax.ShapeDtypeStruct((192, 1024), bf),
        in_specs=[anyspace, anyspace, anyspace, vmem],
        out_specs=vmem,
        scratch_shapes=[
            pltpu.VMEM((2, 16, 192, 512), bf),
            pltpu.VMEM((8, 1024, 384), bf),
            pltpu.VMEM((3072, 512), bf),
            pltpu.VMEM((2, 1024, 512), f32),
            pltpu.VMEM((2, 512, 512), bf),
            pltpu.VMEM((2, 1, 512), f32),
            pltpu.VMEM((2, 6, 2, 192, 512), bf),
            pltpu.VMEM((2, 6, 2, 192, 512), bf),
            pltpu.VMEM((2, 4, 192, 512), bf),
            pltpu.VMEM((2, 2, 96, 512), bf),
            pltpu.VMEM((2, 6, 96, 512), bf),
            dma((4,)),
            dma((2, 20)),
            dma((2, 20)),
            dma((2, 6, 2)),
            dma((2, 6, 2)),
            dma((2, 6)),
            dma((2, 6)),
        ],
        compiler_params=pltpu.CompilerParams(
            collective_id=0, has_side_effects=True, vmem_limit_bytes=60 * 1024 * 1024
        ),
        name="mlp",
    )(stream_t, weights, down_t, gain)


def body(
    dealing,
    residual,
    queries,
    draft_keys,
    draft_values,
    cache_keys,
    cache_values,
    cache_lengths,
    parents,
    draft_counts,
    accepted,
    out_weight,
    norm_gain,
    gate_weight,
    up_weight,
    down_weight,
):
    columns = lax.axis_size("col")
    dealt_order = dealing[0]
    rows_here = residual.shape[0]
    draft_rows = rows_here // columns

    def to_slots(block_rows):
        shaped = block_rows.reshape(columns, draft_rows, block_rows.shape[1])
        return jnp.take(shaped, dealt_order, axis=0).reshape(rows_here, block_rows.shape[1])

    mine_q, mine_k, mine_v = (
        lax.all_to_all(to_slots(queries), "col", split_axis=0, concat_axis=1, tiled=True),
        lax.all_to_all(to_slots(draft_keys), "col", split_axis=0, concat_axis=1, tiled=True),
        lax.all_to_all(to_slots(draft_values), "col", split_axis=0, concat_axis=1, tiled=True),
    )
    attended, new_keys, new_values = verify_slot(
        mine_q,
        mine_k,
        mine_v,
        cache_keys[0],
        cache_values[0],
        cache_lengths[0],
        parents[0],
        draft_counts[0],
        accepted[0],
    )
    wo_t = lax.all_gather(out_weight.T[None], "row", axis=0, tiled=True)
    gate_up = lax.all_gather(
        jnp.concatenate([gate_weight.T, up_weight.T], axis=0)[None], "row", axis=0, tiled=True
    )
    down_t = lax.all_gather(down_weight.T, "row", axis=0, tiled=True)
    gain = lax.all_gather(norm_gain, "col", axis=0, tiled=True).reshape(8, 1, 384)
    every = lax.all_gather(attended, "col", axis=0, tiled=True)
    projected = lax.dot_general(
        jnp.transpose(wo_t, (1, 0, 2)).reshape(192, 3072),
        every,
        (((1,), (1,)), ((), ())),
        preferred_element_type=jnp.float32,
    )
    stream_t = (to_slots(residual).T.astype(jnp.float32) + projected).astype(jnp.bfloat16)
    out_t = mlp_call(stream_t, gate_up, down_t, gain)
    inverse = jnp.argsort(dealt_order)
    layer_out = jnp.take(out_t.T.reshape(columns, draft_rows, 192), inverse, axis=0).reshape(
        rows_here, 192
    )
    return (layer_out, new_keys[None], new_values[None])


def solution(mesh):
    placed = (
        P("row", None),
        P("row", "col"),
        P("row", "col"),
        P("row", "col"),
        P("row", "col"),
        P(("row", "col"), None, None),
        P(("row", "col"), None, None),
        P(("row", "col")),
        P(("row", "col"), None),
        P(("row", "col")),
        P(("row", "col"), None),
        P("row", "col"),
        P("col"),
        P("row", "col"),
        P("row", "col"),
        P("col", "row"),
    )
    return jax.shard_map(
        body,
        mesh=mesh,
        in_specs=placed,
        out_specs=(P("row", "col"), P(("row", "col"), None, None), P(("row", "col"), None, None)),
        check_vma=False,
    )
```

```python
import math

import jax
import jax.numpy as jnp
import numpy as np
from jax import lax
from jax.experimental import pallas as pl
from jax.experimental.pallas import tpu as pltpu
from jax.sharding import PartitionSpec as P

D = 3072
HEAD_DIM = 96
MESH = pl.DeviceIdType.MESH

OFFS = (0, -1, 1, 2)
HOPS = [
    ((0, 0), 1, 1, None, (-1, 0)),
    ((0, 0), 1, -1, None, (1, 0)),
    ((-1, 0), 1, 1, 0, (2, 0)),
    ((1, 0), 1, -1, 1, (2, 0)),
]
for _d in OFFS:
    HOPS += [
        ((_d, 0), 2, 1, None, (_d, -1)),
        ((_d, 0), 2, -1, None, (_d, 1)),
        ((_d, -1), 2, 1, 0, (_d, 2)),
        ((_d, 1), 2, -1, 1, (_d, 2)),
    ]


def attend_kernel(
    dealt_ref, length_ref, count_ref, parent_ref, path_ref, freq_ref, gain_ref,
    q_ref, k_ref, v_ref, res_ref, wo_ref, gate_ref, up_ref, down_ref, ck_hbm, cv_hbm,
    stream_ref, nk_ref, nv_ref, gains_ref, gu_out, dn_out,
    KC, VC, SB, RB, ATT, PA, WO, TG, TD, turn, cosine, sine, anc_ref, RT,
    kv_sem, loc_sem, x_send, x_recv, n_send, n_recv, w_send, w_recv, a_send, a_recv,
):
    f32, bf = jnp.float32, jnp.bfloat16
    row = lax.axis_index("row")
    me = lax.axis_index("col")
    z, x = me // 4, me % 4
    y, core = row // 2, row % 2

    def cache_in(p):
        lanes = pl.ds(pl.multiple_of(p * 384, 128), 384)
        return (
            pltpu.make_async_copy(ck_hbm.at[0, :, lanes], KC.at[p], kv_sem.at[0, p]),
            pltpu.make_async_copy(cv_hbm.at[0, :, lanes], VC.at[p], kv_sem.at[1, p]),
        )

    @pl.loop(0, 8)
    def _(p):
        for c in cache_in(p):
            c.start()

    barrier = pltpu.get_barrier_semaphore()

    @pl.loop(1, 16)
    def _(d):
        pl.semaphore_signal(
            barrier, inc=1, device_id={"col": (me + d) % 16}, device_id_type=MESH
        )

    row_up = ((y + 1) % 4) * 2 + core
    row_down = ((y + 3) % 4) * 2 + core
    row_twin = y * 2 + 1 - core
    for r in (row_up, row_down, row_twin):
        pl.semaphore_signal(barrier, inc=1, device_id={"row": r}, device_id_type=MESH)

    @pl.loop(0, 16)
    def _(j):
        d = dealt_ref[0, j]
        SB[j] = jnp.concatenate(
            [q_ref[d], k_ref[d], v_ref[d], jnp.zeros((64, 64), bf)], axis=1
        )

    gains_ref[me] = gain_ref[...].astype(f32)
    pl.semaphore_wait(barrier, 18)

    def block_copy(j):
        return pltpu.make_async_remote_copy(
            src_ref=SB.at[j], dst_ref=RB.at[me], send_sem=x_send.at[j], recv_sem=x_recv.at[me],
            device_id={"col": j}, device_id_type=MESH,
        )

    def block_arrival(s):
        return pltpu.make_async_remote_copy(
            src_ref=SB.at[s], dst_ref=RB.at[s], send_sem=x_send.at[s], recv_sem=x_recv.at[s],
            device_id={"col": s}, device_id_type=MESH,
        )

    def gain_copy(j, slot):
        return pltpu.make_async_remote_copy(
            src_ref=gains_ref.at[me], dst_ref=gains_ref.at[slot],
            send_sem=n_send.at[j], recv_sem=n_recv.at[slot],
            device_id={"col": j}, device_id_type=MESH,
        )

    RB[me] = SB[me]

    @pl.loop(1, 16)
    def _(d):
        j = (me + d) % 16
        block_copy(j).start()
        gain_copy(j, me).start()

    WO[row] = wo_ref[...].astype(f32).T.astype(bf)
    TG[0:512] = gate_ref[...].astype(f32).T.astype(bf)
    TG[512:1024] = up_ref[...].astype(f32).T.astype(bf)
    TD[...] = down_ref[...].astype(f32).T.astype(bf)
    own_gu = pltpu.make_async_copy(TG, gu_out.at[row], loc_sem.at[0])
    own_dn = pltpu.make_async_copy(TD, dn_out.at[row], loc_sem.at[1])
    own_gu.start()
    own_dn.start()
    tables = ((WO, None, 192), (gu_out, TG, 1024), (dn_out, TD, 384))
    yb = {
        0: row, -1: row_down, 1: row_up, 2: ((y + 2) % 4) * 2 + core,
    }
    wmoves = [
        (0, None, row_up, -1, False),
        (0, None, row_down, 1, False),
        (-1, 0, row_up, 2, False),
        (1, 1, row_down, 2, False),
        (0, None, row_twin, 0, True),
        (-1, None, row_twin, -1, True),
        (1, None, row_twin, 1, True),
        (2, None, row_twin, 2, True),
    ]

    def wref(t, index, part, own):
        table, mine, size = tables[t]
        if own and mine is not None:
            return mine
        if part is None:
            return table.at[index]
        return table.at[index, pl.ds(part * (size // 2), size // 2)]

    def wmove(t, k):
        d, part, target, _, _ = wmoves[k]
        return pltpu.make_async_remote_copy(
            src_ref=wref(t, yb[d], part, d == 0), dst_ref=wref(t, yb[d], part, False),
            send_sem=w_send.at[t, k], recv_sem=w_recv.at[t, k],
            device_id={"row": target}, device_id_type=MESH,
        )

    def wgot(t, k):
        _, part, target, d, twin = wmoves[k]
        index = yb[d] + 1 - 2 * core if twin else yb[d]
        ref = wref(t, index, part, False)
        pltpu.make_async_remote_copy(
            src_ref=ref, dst_ref=ref, send_sem=w_send.at[t, k], recv_sem=w_recv.at[t, k],
            device_id={"row": target}, device_id_type=MESH,
        ).wait_recv()

    for t in range(3):
        for k in (0, 1, 4):
            wmove(t, k).start()

    i64 = lax.broadcasted_iota(jnp.int32, (64, 64), 0)
    j64 = lax.broadcasted_iota(jnp.int32, (64, 64), 1)
    anc = jnp.logical_or(parent_ref[...] == j64, i64 == j64).astype(f32)
    for sweep in range(6):
        half = anc.astype(bf)
        anc = jnp.minimum(jnp.dot(half, half, preferred_element_type=f32), 1.0)
    length = length_ref[0]
    live = count_ref[0]
    position = length.astype(f32) + jnp.sum(anc, axis=1, keepdims=True) - 1.0
    angle = position * freq_ref[...]
    cosine[...] = jnp.cos(angle)
    sine[...] = jnp.sin(angle)
    anc_ref[...] = jnp.where(j64 < live, anc, 0.0)
    ti = lax.broadcasted_iota(jnp.int32, (192, 192), 0)
    tj = lax.broadcasted_iota(jnp.int32, (192, 192), 1)
    low = (tj % 96) < 48
    turn[...] = jnp.where(
        jnp.logical_and(low, ti == tj + 48), -1.0,
        jnp.where(jnp.logical_and(jnp.logical_not(low), ti == tj - 48), 1.0, 0.0),
    ).astype(bf)

    @pl.loop(0, 8)
    def _(m):
        pair = jnp.concatenate(
            [res_ref[dealt_ref[0, 2 * m]], res_ref[dealt_ref[0, 2 * m + 1]]], axis=0
        ).astype(f32)
        RT[:, pl.ds(pl.multiple_of(m * 128, 128), 128)] = pair.T

    def rotated(rows):
        swapped = jnp.dot(rows, turn[...], preferred_element_type=f32)
        return (rows.astype(f32) * cosine[...] + swapped * sine[...]).astype(bf)

    a_own, b_own = (x, z), (z, x)

    def at(h, da, db):
        a, b = (a_own[h] + da + 4) % 4, (b_own[h] + db + 4) % 4
        return b * 4 + a if h == 0 else a * 4 + b

    def piece(p, c, part):
        return ATT.at[p, c] if part is None else ATT.at[p, c, pl.ds(32 * part, 32)]

    def amove(p, h, k):
        (da, db), axis, way, part, _ = HOPS[k]
        ref = piece(p, at(h, da, db), part)
        target = at(h, way, 0) if axis == 1 else at(h, 0, way)
        return pltpu.make_async_remote_copy(
            src_ref=ref, dst_ref=ref, send_sem=a_send.at[p, k], recv_sem=a_recv.at[p, k],
            device_id={"col": target}, device_id_type=MESH,
        )

    def agot(p, h, k):
        _, axis, way, part, (da, db) = HOPS[k]
        ref = piece(p, at(h, da, db), part)
        target = at(h, way, 0) if axis == 1 else at(h, 0, way)
        pltpu.make_async_remote_copy(
            src_ref=ref, dst_ref=ref, send_sem=a_send.at[p, k], recv_sem=a_recv.at[p, k],
            device_id={"col": target}, device_id_type=MESH,
        ).wait_recv()

    nt = (((1,), (1,)), ((), ()))
    scale = 1.0 / math.sqrt(HEAD_DIM)
    head_of_lane = lax.broadcasted_iota(jnp.int32, (64, 384), 1) // 96
    key_live = lax.broadcasted_iota(jnp.int32, (1, 1536), 1) < length
    path_hot = (
        path_ref[...] == lax.broadcasted_iota(jnp.int32, (8, 64), 1)
    ).astype(f32).astype(bf)

    def chunk(p, h):
        for e in range(2):
            @pl.when(2 * p + e != me)
            def _(e=e):
                block_arrival(2 * p + e).wait_recv()
        first, other = RB[2 * p], RB[2 * p + 1]
        q = jnp.concatenate([rotated(first[:, 0:192]), rotated(other[:, 0:192])], axis=1)
        kd = jnp.concatenate([rotated(first[:, 192:384]), rotated(other[:, 192:384])], axis=1)
        vd = jnp.concatenate([first[:, 384:576], other[:, 384:576]], axis=1)
        lanes = pl.ds(pl.multiple_of(p * 384, 128), 384)
        nk_ref[0, :, lanes] = jnp.dot(path_hot, kd, preferred_element_type=f32).astype(bf)
        nv_ref[0, :, lanes] = jnp.dot(path_hot, vd, preferred_element_type=f32).astype(bf)
        wide = jnp.concatenate(
            [jnp.where(head_of_lane == n, q, jnp.zeros_like(q)) for n in range(4)], axis=0
        )
        for c in cache_in(p):
            c.wait()
        old = lax.dot_general(wide, KC[p], nt, preferred_element_type=f32)
        old = jnp.where(key_live, old, -jnp.inf)
        new = lax.dot_general(wide, kd, nt, preferred_element_type=f32)
        allowed = jnp.concatenate([anc_ref[...]] * 4, axis=0) > 0.5
        new = jnp.where(allowed, new, -jnp.inf)
        top = jnp.maximum(
            jnp.max(old, axis=1, keepdims=True), jnp.max(new, axis=1, keepdims=True)
        )
        w_old = jnp.exp((old - top) * scale)
        w_new = jnp.exp((new - top) * scale)
        total = jnp.sum(w_old, axis=1, keepdims=True) + jnp.sum(w_new, axis=1, keepdims=True)
        mixed = jnp.dot(w_old.astype(bf), VC[p], preferred_element_type=f32) + jnp.dot(
            w_new.astype(bf), vd, preferred_element_type=f32
        )
        mixed = mixed / total
        attended = jnp.zeros((64, 384), f32)
        for n in range(4):
            attended = jnp.where(head_of_lane == n, mixed[64 * n : 64 * n + 64], attended)
        ATT[p, me] = attended.astype(bf)
        for k in (0, 1, 4, 5):
            amove(p, h, k).start()

    @pl.loop(0, 4)
    def _(g):
        for h in range(2):
            chunk(2 * g + h, h)

    def forward(t):
        wgot(t, 0)
        wmove(t, 2).start()
        wmove(t, 5).start()
        wgot(t, 1)
        wmove(t, 3).start()
        wmove(t, 6).start()

    def last(t):
        wgot(t, 2)
        wgot(t, 3)
        wmove(t, 7).start()

    def stage(moves):
        @pl.loop(0, 4)
        def _(g):
            for h in range(2):
                for waits, starts in moves:
                    for k in waits:
                        agot(2 * g + h, h, k)
                    for k in starts:
                        amove(2 * g + h, h, k).start()

    forward(0)
    stage([((0,), (2, 8, 9)), ((1,), (3, 12, 13))])
    forward(1)
    stage([((4,), (6,)), ((5,), (7,)), ((2, 3), (16, 17))])
    last(0)
    forward(2)
    stage([((8,), (10,)), ((9,), (11,)), ((12,), (14,)), ((13,), (15,))])
    stage([((16,), (18,)), ((17,), (19,))])
    last(1)
    PA[...] = RT[...]
    for k in (4, 5, 6, 7):
        wgot(0, k)

    @pl.loop(0, 4)
    def _(g):
        for h in range(2):
            p = 2 * g + h
            for k in (6, 7, 10, 11, 14, 15, 18, 19):
                agot(p, h, k)
            PA[...] += lax.dot_general(
                WO[p], ATT[p].reshape(1024, 384), nt, preferred_element_type=f32
            )

    stream_ref[...] = PA[...].astype(bf)
    last(2)
    for t in (1, 2):
        for k in (4, 5, 6, 7):
            wgot(t, k)

    @pl.loop(1, 16)
    def _(d):
        j = (me + d) % 16
        block_copy(j).wait_send()
        gain_copy(j, me).wait_send()
        gain_copy(j, j).wait_recv()

    for t in range(3):
        for k in range(8):
            wmove(t, k).wait_send()

    @pl.loop(0, 4)
    def _(g):
        for h in range(2):
            for k in range(20):
                amove(2 * g + h, h, k).wait_send()

    own_gu.wait()
    own_dn.wait()


def attend_call(dealing, lengths, counts, parent_col, path_col, freq, gain, q, k, v, res, wo, gate, up, down, ck, cv):
    anyspace = pl.BlockSpec(memory_space=pl.ANY)
    vmem = pl.BlockSpec(memory_space=pltpu.VMEM)
    smem = pl.BlockSpec(memory_space=pltpu.SMEM)
    bf, f32 = jnp.bfloat16, jnp.float32
    dma = pltpu.SemaphoreType.DMA
    return pl.pallas_call(
        attend_kernel,
        out_shape=(
            jax.ShapeDtypeStruct((192, 1024), bf),
            jax.ShapeDtypeStruct((1, 8, 3072), bf),
            jax.ShapeDtypeStruct((1, 8, 3072), bf),
            jax.ShapeDtypeStruct((16, 1, 192), f32),
            jax.ShapeDtypeStruct((8, 1024, 384), bf),
            jax.ShapeDtypeStruct((8, 384, 512), bf),
        ),
        in_specs=[smem] * 3 + [vmem] * 12 + [anyspace] * 2,
        out_specs=(vmem, vmem, vmem, vmem, anyspace, anyspace),
        scratch_shapes=[
            pltpu.VMEM((8, 1536, 384), bf),
            pltpu.VMEM((8, 1536, 384), bf),
            pltpu.VMEM((16, 64, 640), bf),
            pltpu.VMEM((16, 64, 640), bf),
            pltpu.VMEM((8, 16, 64, 384), bf),
            pltpu.VMEM((192, 1024), f32),
            pltpu.VMEM((8, 192, 384), bf),
            pltpu.VMEM((1024, 384), bf),
            pltpu.VMEM((384, 512), bf),
            pltpu.VMEM((192, 192), bf),
            pltpu.VMEM((64, 192), f32),
            pltpu.VMEM((64, 192), f32),
            pltpu.VMEM((64, 64), f32),
            pltpu.VMEM((192, 1024), f32),
            dma((2, 8)),
            dma((2,)),
            dma((16,)),
            dma((16,)),
            dma((16,)),
            dma((16,)),
            dma((3, 8)),
            dma((3, 8)),
            dma((8, 20)),
            dma((8, 20)),
        ],
        compiler_params=pltpu.CompilerParams(
            collective_id=1, has_side_effects=True, vmem_limit_bytes=60 * 1024 * 1024
        ),
        name="attend",
    )(dealing, lengths, counts, parent_col, path_col, freq, gain, q, k, v, res, wo, gate, up, down, ck, cv)


def mlp_kernel(
    st_hbm, w_hbm, dn_hbm, gain_ref, out_ref,
    S, W, DN, acc, H, ss, T, R, Q, T2, R2,
    loc_sem, ag_send, ag_recv, rs_send, rs_recv, rt_send, rt_recv,
):
    me = lax.axis_index("col")
    z, x = me // 4, me % 4
    halves = (0, 1)
    a_own, b_own = (x, z), (z, x)

    def blk(h, a, b):
        return b * 4 + a if h == 0 else a * 4 + b

    def peer1(h, d):
        return blk(h, (a_own[h] + d + 4) % 4, b_own[h])

    def peer2(h, d):
        return blk(h, a_own[h], (b_own[h] + d + 4) % 4)

    stream_in = [
        pltpu.make_async_copy(st_hbm.at[:, pl.ds(512 * h, 512)], S.at[h, me], loc_sem.at[h])
        for h in halves
    ]
    w_in = pltpu.make_async_copy(w_hbm, W, loc_sem.at[2])
    dn_in = pltpu.make_async_copy(dn_hbm, DN, loc_sem.at[3])
    for c in stream_in:
        c.start()
    w_in.start()
    dn_in.start()

    barrier = pltpu.get_barrier_semaphore()
    for p in (peer1(0, 1), peer1(0, -1), peer1(1, 1), peer1(1, -1)):
        pl.semaphore_signal(barrier, inc=1, device_id={"col": p}, device_id_type=MESH)
    pl.semaphore_wait(barrier, 4)
    for c in stream_in:
        c.wait()

    sent = []

    def push(h, k, c, target, rows=None):
        ref = S.at[h, c] if rows is None else S.at[h, c, pl.ds(rows, 96)]
        cp = pltpu.make_async_remote_copy(
            src_ref=ref, dst_ref=ref, send_sem=ag_send.at[h, k], recv_sem=ag_recv.at[h, k],
            device_id={"col": target}, device_id_type=MESH,
        )
        cp.start()
        sent.append(cp)

    def arrived(h, k, c, rows=None):
        ref = S.at[h, c] if rows is None else S.at[h, c, pl.ds(rows, 96)]
        pltpu.make_async_remote_copy(
            src_ref=ref, dst_ref=ref, send_sem=ag_send.at[h, k], recv_sem=ag_recv.at[h, k],
            device_id={"col": me}, device_id_type=MESH,
        ).wait_recv()

    def at(h, da, db):
        return blk(h, (a_own[h] + da + 4) % 4, (b_own[h] + db + 4) % 4)

    offs = (0, -1, 1, 2)
    for h in halves:
        push(h, 0, me, peer1(h, 1))
        push(h, 1, me, peer1(h, -1))
    for h in halves:
        push(h, 4, me, peer2(h, 1))
        push(h, 5, me, peer2(h, -1))

    acc[...] = jnp.zeros_like(acc)
    ss[...] = jnp.zeros_like(ss)
    w_in.wait()

    @pl.loop(0, 8)
    def _(r):
        both = jnp.concatenate([gain_ref[2 * r], gain_ref[2 * r + 1]], axis=1)
        W[r] = W[r] * both.astype(jnp.bfloat16)

    for h in halves:
        arrived(h, 0, at(h, -1, 0))
        push(h, 2, at(h, -1, 0), peer1(h, 1), 0)
        push(h, 8, at(h, -1, 0), peer2(h, 1))
        push(h, 9, at(h, -1, 0), peer2(h, -1))
        arrived(h, 1, at(h, 1, 0))
        push(h, 3, at(h, 1, 0), peer1(h, -1), 96)
        push(h, 12, at(h, 1, 0), peer2(h, 1))
        push(h, 13, at(h, 1, 0), peer2(h, -1))

    def second(j):
        for h in halves:
            base = 4 + 4 * j
            arrived(h, base, at(h, offs[j], -1))
            push(h, base + 2, at(h, offs[j], -1), peer2(h, 1), 0)
            arrived(h, base + 1, at(h, offs[j], 1))
            push(h, base + 3, at(h, offs[j], 1), peer2(h, -1), 96)

    def square(h, c):
        v = S[h, c].astype(jnp.float32)
        ss[h] += jnp.sum(v * v, axis=0, keepdims=True)

    def fold_a(zz):
        for i in range(4):
            square(0, zz * 4 + i)
        k0 = S[0, pl.ds(zz * 4, 2)].reshape(384, 512)
        k1 = S[0, pl.ds(zz * 4 + 2, 2)].reshape(384, 512)

        @pl.loop(0, 4)
        def _(m):
            rows = pl.ds(pl.multiple_of(m * 256, 256), 256)
            acc[0, rows] += jnp.dot(
                W[2 * zz, rows], k0, preferred_element_type=jnp.float32
            ) + jnp.dot(W[2 * zz + 1, rows], k1, preferred_element_type=jnp.float32)

    def fold_b(q):
        @pl.loop(0, 2)
        def _(g):
            for i in range(2):
                for e in range(2):
                    square(1, (2 * g + i) * 4 + 2 * q + e)
            k0 = S[1, pl.ds(8 * g + 2 * q, 2)].reshape(384, 512)
            k1 = S[1, pl.ds(8 * g + 4 + 2 * q, 2)].reshape(384, 512)

            @pl.loop(0, 4)
            def _(m):
                rows = pl.ds(pl.multiple_of(m * 256, 256), 256)
                acc[1, rows] += jnp.dot(
                    W[4 * g + q, rows], k0, preferred_element_type=jnp.float32
                ) + jnp.dot(W[4 * g + 2 + q, rows], k1, preferred_element_type=jnp.float32)

    second(0)
    for h in halves:
        arrived(h, 2, at(h, 2, 0), 0)
        arrived(h, 3, at(h, 2, 0), 96)
        push(h, 16, at(h, 2, 0), peer2(h, 1))
        push(h, 17, at(h, 2, 0), peer2(h, -1))
    fold_a(z)
    second(1)
    second(2)
    second(3)

    @pl.loop(0, 2)
    def _(i):
        fold_a((z + 3 + 2 * i) % 4)

    fold_b(x // 2)
    for h in halves:
        for j in range(4):
            arrived(h, 6 + 4 * j, at(h, offs[j], 2), 0)
            arrived(h, 7 + 4 * j, at(h, offs[j], 2), 96)
    fold_a((z + 2) % 4)
    fold_b(1 - x // 2)
    for cp in sent:
        cp.wait_send()

    for h in halves:
        factor = lax.rsqrt(ss[h] * (1.0 / D) + 1e-05)

        @pl.loop(0, 4)
        def _(m, h=h, factor=factor):
            rows = pl.ds(pl.multiple_of(m * 128, 128), 128)
            uprows = pl.ds(pl.multiple_of(512 + m * 128, 128), 128)
            g = acc[h, rows] * factor
            u = acc[h, uprows] * factor
            H[h, rows] = (g / (1.0 + jnp.exp(-g)) * u).astype(jnp.bfloat16)

    dn_in.wait()

    def part(h, c):
        rows = pl.ds(pl.multiple_of(c * 192, 192), 192)
        return jnp.dot(DN[rows], H[h], preferred_element_type=jnp.float32)

    sent = []

    def send1(h, kind, i):
        d = 1 if kind % 2 == 0 else -1
        cp = pltpu.make_async_remote_copy(
            src_ref=T.at[h, kind, i], dst_ref=R.at[h, kind, i],
            send_sem=rs_send.at[h, kind, i], recv_sem=rs_recv.at[h, kind, i],
            device_id={"col": peer1(h, d)}, device_id_type=MESH,
        )
        cp.start()
        sent.append(cp)

    def got1(h, kind, i):
        pltpu.make_async_remote_copy(
            src_ref=T.at[h, kind, i], dst_ref=R.at[h, kind, i],
            send_sem=rs_send.at[h, kind, i], recv_sem=rs_recv.at[h, kind, i],
            device_id={"col": me}, device_id_type=MESH,
        ).wait_recv()

    def dest(h, da, b):
        return blk(h, (a_own[h] + da + 4) % 4, b)

    for kind, da, b0 in ((0, 2, 0), (1, 2, 2), (4, 1, 2), (5, -1, 0)):
        for i in range(2):
            for h in halves:
                T[h, kind, i] = part(h, dest(h, da, b0 + i)).astype(jnp.bfloat16)
                send1(h, kind, i)
    for kind, da, b0 in ((2, 1, 0), (3, -1, 2)):
        for i in range(2):
            for h in halves:
                mine = part(h, dest(h, da, b0 + i))
                got1(h, kind - 2, i)
                T[h, kind, i] = (mine + R[h, kind - 2, i].astype(jnp.float32)).astype(jnp.bfloat16)
                send1(h, kind, i)
    for b in range(4):
        for h in halves:
            mine = part(h, dest(h, 0, b))
            s_kind, d_kind = (2, 5) if b < 2 else (3, 4)
            got1(h, s_kind, b % 2)
            got1(h, d_kind, b % 2)
            Q[h, b] = (
                mine
                + R[h, s_kind, b % 2].astype(jnp.float32)
                + R[h, d_kind, b % 2].astype(jnp.float32)
            ).astype(jnp.bfloat16)
    for h in halves:
        for i in range(2):
            pass

    def copy2(h, kind, src, target):
        return pltpu.make_async_remote_copy(
            src_ref=src, dst_ref=R2.at[h, kind],
            send_sem=rt_send.at[h, kind], recv_sem=rt_recv.at[h, kind],
            device_id={"col": target}, device_id_type=MESH,
        )

    def bmod(h, d):
        return (b_own[h] + d + 4) % 4

    for h in halves:
        for kind, d, row in ((0, 2, 0), (1, 2, 96), (4, 1, 96), (5, -1, 0)):
            cp = copy2(h, kind, Q.at[h, bmod(h, d), pl.ds(row, 96)], peer2(h, 1 if kind % 2 == 0 else -1))
            cp.start()
            sent.append(cp)
    for h in halves:
        for kind, d, row in ((2, 1, 0), (3, -1, 96)):
            copy2(h, kind - 2, T2.at[h, 0], me).wait_recv()
            T2[h, kind - 2] = (
                Q[h, bmod(h, d), pl.ds(row, 96)].astype(jnp.float32)
                + R2[h, kind - 2].astype(jnp.float32)
            ).astype(jnp.bfloat16)
            cp = copy2(h, kind, T2.at[h, kind - 2], peer2(h, 1 if kind == 2 else -1))
            cp.start()
            sent.append(cp)
    for h in halves:
        for row, s_kind, d_kind in ((0, 2, 5), (96, 3, 4)):
            copy2(h, s_kind, T2.at[h, 0], me).wait_recv()
            copy2(h, d_kind, T2.at[h, 0], me).wait_recv()
            out_ref[pl.ds(row, 96), pl.ds(512 * h, 512)] = (
                S[h, me, pl.ds(row, 96)].astype(jnp.float32)
                + Q[h, b_own[h], pl.ds(row, 96)].astype(jnp.float32)
                + R2[h, s_kind].astype(jnp.float32)
                + R2[h, d_kind].astype(jnp.float32)
            ).astype(jnp.bfloat16)
    for cp in sent:
        cp.wait_send()


def mlp_call(stream_t, weights, down_t, gain):
    anyspace = pl.BlockSpec(memory_space=pl.ANY)
    vmem = pl.BlockSpec(memory_space=pltpu.VMEM)
    bf, f32 = jnp.bfloat16, jnp.float32
    dma = pltpu.SemaphoreType.DMA
    return pl.pallas_call(
        mlp_kernel,
        out_shape=jax.ShapeDtypeStruct((192, 1024), bf),
        in_specs=[anyspace, anyspace, anyspace, vmem],
        out_specs=vmem,
        scratch_shapes=[
            pltpu.VMEM((2, 16, 192, 512), bf),
            pltpu.VMEM((8, 1024, 384), bf),
            pltpu.VMEM((3072, 512), bf),
            pltpu.VMEM((2, 1024, 512), f32),
            pltpu.VMEM((2, 512, 512), bf),
            pltpu.VMEM((2, 1, 512), f32),
            pltpu.VMEM((2, 6, 2, 192, 512), bf),
            pltpu.VMEM((2, 6, 2, 192, 512), bf),
            pltpu.VMEM((2, 4, 192, 512), bf),
            pltpu.VMEM((2, 2, 96, 512), bf),
            pltpu.VMEM((2, 6, 96, 512), bf),
            dma((4,)),
            dma((2, 20)),
            dma((2, 20)),
            dma((2, 6, 2)),
            dma((2, 6, 2)),
            dma((2, 6)),
            dma((2, 6)),
        ],
        compiler_params=pltpu.CompilerParams(
            collective_id=0, has_side_effects=True, vmem_limit_bytes=60 * 1024 * 1024
        ),
        name="mlp",
    )(stream_t, weights, down_t, gain)


def body(
    dealing,
    residual,
    queries,
    draft_keys,
    draft_values,
    cache_keys,
    cache_values,
    cache_lengths,
    parents,
    draft_counts,
    accepted,
    out_weight,
    norm_gain,
    gate_weight,
    up_weight,
    down_weight,
):
    freq = np.power(10000.0, -(np.arange(192) % 48) * (2.0 / HEAD_DIM)).astype(np.float32)

    def by_request(rows):
        return rows.reshape(16, 64, 192)

    stream_t, new_keys, new_values, gains, gate_up, down_t = attend_call(
        dealing,
        cache_lengths,
        draft_counts,
        parents.reshape(64, 1),
        accepted.reshape(8, 1),
        jnp.asarray(freq).reshape(1, 192),
        norm_gain.reshape(1, 192),
        by_request(queries),
        by_request(draft_keys),
        by_request(draft_values),
        by_request(residual),
        out_weight,
        gate_weight,
        up_weight,
        down_weight,
        cache_keys,
        cache_values,
    )
    out_t = mlp_call(stream_t, gate_up, down_t.reshape(3072, 512), gains)
    inverse = jnp.argsort(dealing[0])
    layer_out = jnp.take(out_t.T.reshape(16, 64, 192), inverse, axis=0).reshape(1024, 192)
    return (layer_out, new_keys, new_values)


def solution(mesh):
    placed = (
        P("row", None),
        P("row", "col"),
        P("row", "col"),
        P("row", "col"),
        P("row", "col"),
        P(("row", "col"), None, None),
        P(("row", "col"), None, None),
        P(("row", "col")),
        P(("row", "col"), None),
        P(("row", "col")),
        P(("row", "col"), None),
        P("row", "col"),
        P("col"),
        P("row", "col"),
        P("row", "col"),
        P("col", "row"),
    )
    return jax.shard_map(
        body,
        mesh=mesh,
        in_specs=placed,
        out_specs=(P("row", "col"), P(("row", "col"), None, None), P(("row", "col"), None, None)),
        check_vma=False,
    )
```

```python
import math

import jax
import jax.numpy as jnp
import numpy as np
from jax import lax
from jax.experimental import pallas as pl
from jax.experimental.pallas import tpu as pltpu
from jax.sharding import PartitionSpec as P

D = 3072
HEAD_DIM = 96
MESH = pl.DeviceIdType.MESH

OFFS = (0, -1, 1, 2)
HOPS = [
    ((0, 0), 1, 1, None, (-1, 0)),
    ((0, 0), 1, -1, None, (1, 0)),
    ((-1, 0), 1, 1, 0, (2, 0)),
    ((1, 0), 1, -1, 1, (2, 0)),
]
for _d in OFFS:
    HOPS += [
        ((_d, 0), 2, 1, None, (_d, -1)),
        ((_d, 0), 2, -1, None, (_d, 1)),
        ((_d, -1), 2, 1, 0, (_d, 2)),
        ((_d, 1), 2, -1, 1, (_d, 2)),
    ]


def attend_kernel(
    dealt_ref, length_ref, count_ref, parent_ref, path_ref, freq_ref, gain_ref,
    q_ref, k_ref, v_ref, res_ref, wo_ref, gate_ref, up_ref, down_ref, ck_hbm, cv_hbm,
    stream_ref, nk_ref, nv_ref, gains_ref, gu_out, dn_out,
    KC, VC, SB, RB, ATT, PA, WO, TG, TD, turn, cosine, sine, anc_ref, TT, RB1,
    kv_sem, loc_sem, x_send, x_recv, n_send, n_recv, w_send, w_recv, a_send, a_recv,
):
    f32, bf = jnp.float32, jnp.bfloat16
    row = lax.axis_index("row")
    me = lax.axis_index("col")
    z, x = me // 4, me % 4
    y, core = row // 2, row % 2

    def cache_in(p):
        lanes = pl.ds(pl.multiple_of(p * 384, 128), 384)
        return (
            pltpu.make_async_copy(ck_hbm.at[0, :, lanes], KC.at[p], kv_sem.at[0, p]),
            pltpu.make_async_copy(cv_hbm.at[0, :, lanes], VC.at[p], kv_sem.at[1, p]),
        )

    @pl.loop(0, 8)
    def _(p):
        for c in cache_in(p):
            c.start()

    barrier = pltpu.get_barrier_semaphore()

    @pl.loop(1, 16)
    def _(d):
        pl.semaphore_signal(
            barrier, inc=1, device_id={"col": (me + d) % 16}, device_id_type=MESH
        )

    row_up = ((y + 1) % 4) * 2 + core
    row_down = ((y + 3) % 4) * 2 + core
    row_twin = y * 2 + 1 - core
    for r in (row_up, row_down, row_twin):
        pl.semaphore_signal(barrier, inc=1, device_id={"row": r}, device_id_type=MESH)

    for n, ref in enumerate((q_ref, k_ref, v_ref)):
        for m in range(4):
            rows = ref[:, 256 * m : 256 * m + 256].astype(f32).T.astype(bf)
            TT[4 * m : 4 * m + 4, :, 192 * n : 192 * n + 192] = rows.reshape(4, 64, 192)

    @pl.loop(0, 16)
    def _(j):
        block = TT[dealt_ref[0, j]]
        for n in range(4):
            SB[j, 64 * n : 64 * n + 64] = block[:, 128 * n : 128 * n + 128]
        SB[j, 256:288] = jnp.concatenate([block[0:32, 512:576], block[32:64, 512:576]], axis=1)

    gains_ref[me] = gain_ref[...].astype(f32).reshape(1, 192)
    pl.semaphore_wait(barrier, 18)

    def block_copy(j):
        return pltpu.make_async_remote_copy(
            src_ref=SB.at[j], dst_ref=RB.at[me], send_sem=x_send.at[j], recv_sem=x_recv.at[me],
            device_id={"col": j}, device_id_type=MESH,
        )

    def block_arrival(s):
        return pltpu.make_async_remote_copy(
            src_ref=SB.at[s], dst_ref=RB.at[s], send_sem=x_send.at[s], recv_sem=x_recv.at[s],
            device_id={"col": s}, device_id_type=MESH,
        )

    def gain_copy(j, slot):
        return pltpu.make_async_remote_copy(
            src_ref=gains_ref.at[me], dst_ref=gains_ref.at[slot],
            send_sem=n_send.at[j], recv_sem=n_recv.at[slot],
            device_id={"col": j}, device_id_type=MESH,
        )

    RB[me] = SB[me]

    @pl.loop(1, 16)
    def _(d):
        j = (me + d) % 16
        block_copy(j).start()
        gain_copy(j, me).start()

    WO[row] = wo_ref[...]
    TG[0:512] = gate_ref[...].astype(f32).T.astype(bf)
    TG[512:1024] = up_ref[...].astype(f32).T.astype(bf)
    TD[...] = down_ref[...].astype(f32).T.astype(bf)
    own_gu = pltpu.make_async_copy(TG, gu_out.at[row], loc_sem.at[0])
    own_dn = pltpu.make_async_copy(TD, dn_out.at[row], loc_sem.at[1])
    own_gu.start()
    own_dn.start()
    tables = ((WO, None, 192), (gu_out, TG, 1024), (dn_out, TD, 384))
    yb = {
        0: row, -1: row_down, 1: row_up, 2: ((y + 2) % 4) * 2 + core,
    }
    wmoves = [
        (0, None, row_up, -1, False),
        (0, None, row_down, 1, False),
        (-1, 0, row_up, 2, False),
        (1, 1, row_down, 2, False),
        (0, None, row_twin, 0, True),
        (-1, None, row_twin, -1, True),
        (1, None, row_twin, 1, True),
        (2, None, row_twin, 2, True),
    ]

    def wref(t, index, part, own):
        table, mine, size = tables[t]
        if own and mine is not None:
            return mine
        if part is None:
            return table.at[index]
        return table.at[index, pl.ds(part * (size // 2), size // 2)]

    def wmove(t, k):
        d, part, target, _, _ = wmoves[k]
        return pltpu.make_async_remote_copy(
            src_ref=wref(t, yb[d], part, d == 0), dst_ref=wref(t, yb[d], part, False),
            send_sem=w_send.at[t, k], recv_sem=w_recv.at[t, k],
            device_id={"row": target}, device_id_type=MESH,
        )

    def wgot(t, k):
        _, part, target, d, twin = wmoves[k]
        index = yb[d] + 1 - 2 * core if twin else yb[d]
        ref = wref(t, index, part, False)
        pltpu.make_async_remote_copy(
            src_ref=ref, dst_ref=ref, send_sem=w_send.at[t, k], recv_sem=w_recv.at[t, k],
            device_id={"row": target}, device_id_type=MESH,
        ).wait_recv()

    for t in range(3):
        for k in (0, 1, 4):
            wmove(t, k).start()

    i64 = lax.broadcasted_iota(jnp.int32, (64, 64), 0)
    j64 = lax.broadcasted_iota(jnp.int32, (64, 64), 1)
    anc = jnp.logical_or(parent_ref[...] == i64, i64 == j64).astype(f32)
    for sweep in range(6):
        half = anc.astype(bf)
        anc = jnp.minimum(jnp.dot(half, half, preferred_element_type=f32), 1.0)
    anc = anc.T
    length = length_ref[0]
    live = count_ref[0]
    position = length.astype(f32) + jnp.sum(anc, axis=1, keepdims=True) - 1.0
    angle = position * freq_ref[...]
    cosine[...] = jnp.cos(angle)
    sine[...] = jnp.sin(angle)
    anc_ref[...] = jnp.where(j64 < live, anc, 0.0)
    ti = lax.broadcasted_iota(jnp.int32, (192, 192), 0)
    tj = lax.broadcasted_iota(jnp.int32, (192, 192), 1)
    low = (tj % 96) < 48
    turn[...] = jnp.where(
        jnp.logical_and(low, ti == tj + 48), -1.0,
        jnp.where(jnp.logical_and(jnp.logical_not(low), ti == tj - 48), 1.0, 0.0),
    ).astype(bf)

    for j in range(16):
        RB1[j] = res_ref[:, 64 * j : 64 * j + 64]

    @pl.loop(0, 8)
    def _(m):
        pair = jnp.concatenate([RB1[dealt_ref[0, 2 * m]], RB1[dealt_ref[0, 2 * m + 1]]], axis=1)
        PA[:, pl.ds(pl.multiple_of(m * 128, 128), 128)] = pair.astype(f32)

    def rotated(rows):
        swapped = jnp.dot(rows, turn[...], preferred_element_type=f32)
        return (rows.astype(f32) * cosine[...] + swapped * sine[...]).astype(bf)

    a_own, b_own = (x, z), (z, x)

    def at(h, da, db):
        a, b = (a_own[h] + da + 4) % 4, (b_own[h] + db + 4) % 4
        return b * 4 + a if h == 0 else a * 4 + b

    def piece(p, c, part):
        return ATT.at[p, c] if part is None else ATT.at[p, c, pl.ds(32 * part, 32)]

    def amove(p, h, k):
        (da, db), axis, way, part, _ = HOPS[k]
        ref = piece(p, at(h, da, db), part)
        target = at(h, way, 0) if axis == 1 else at(h, 0, way)
        return pltpu.make_async_remote_copy(
            src_ref=ref, dst_ref=ref, send_sem=a_send.at[p, k], recv_sem=a_recv.at[p, k],
            device_id={"col": target}, device_id_type=MESH,
        )

    def agot(p, h, k):
        _, axis, way, part, (da, db) = HOPS[k]
        ref = piece(p, at(h, da, db), part)
        target = at(h, way, 0) if axis == 1 else at(h, 0, way)
        pltpu.make_async_remote_copy(
            src_ref=ref, dst_ref=ref, send_sem=a_send.at[p, k], recv_sem=a_recv.at[p, k],
            device_id={"col": target}, device_id_type=MESH,
        ).wait_recv()

    nt = (((1,), (1,)), ((), ()))
    scale = 1.0 / math.sqrt(HEAD_DIM)
    head_of_lane = lax.broadcasted_iota(jnp.int32, (64, 384), 1) // 96
    key_live = lax.broadcasted_iota(jnp.int32, (1, 1536), 1) < length
    path_hot = (
        (path_ref[...] == lax.broadcasted_iota(jnp.int32, (64, 8), 0)).astype(f32).T.astype(bf)
    )

    def chunk(p, h):
        for e in range(2):
            @pl.when(2 * p + e != me)
            def _(e=e):
                block_arrival(2 * p + e).wait_recv()
        def unpack(s):
            block = RB[s]
            tail = jnp.concatenate([block[256:288, 0:64], block[256:288, 64:128]], axis=0)
            return jnp.concatenate([block[64 * n : 64 * n + 64] for n in range(4)] + [tail], axis=1)

        first, other = unpack(2 * p), unpack(2 * p + 1)
        q = jnp.concatenate([rotated(first[:, 0:192]), rotated(other[:, 0:192])], axis=1)
        kd = jnp.concatenate([rotated(first[:, 192:384]), rotated(other[:, 192:384])], axis=1)
        vd = jnp.concatenate([first[:, 384:576], other[:, 384:576]], axis=1)
        lanes = pl.ds(pl.multiple_of(p * 384, 128), 384)
        nk_ref[0, :, lanes] = jnp.dot(path_hot, kd, preferred_element_type=f32).astype(bf)
        nv_ref[0, :, lanes] = jnp.dot(path_hot, vd, preferred_element_type=f32).astype(bf)
        wide = jnp.concatenate(
            [jnp.where(head_of_lane == n, q, jnp.zeros_like(q)) for n in range(4)], axis=0
        )
        for c in cache_in(p):
            c.wait()
        old = lax.dot_general(wide, KC[p], nt, preferred_element_type=f32)
        old = jnp.where(key_live, old, -jnp.inf)
        new = lax.dot_general(wide, kd, nt, preferred_element_type=f32)
        allowed = jnp.concatenate([anc_ref[...]] * 4, axis=0) > 0.5
        new = jnp.where(allowed, new, -jnp.inf)
        top = jnp.maximum(
            jnp.max(old, axis=1, keepdims=True), jnp.max(new, axis=1, keepdims=True)
        )
        w_old = jnp.exp((old - top) * scale)
        w_new = jnp.exp((new - top) * scale)
        total = jnp.sum(w_old, axis=1, keepdims=True) + jnp.sum(w_new, axis=1, keepdims=True)
        mixed = jnp.dot(w_old.astype(bf), VC[p], preferred_element_type=f32) + jnp.dot(
            w_new.astype(bf), vd, preferred_element_type=f32
        )
        mixed = mixed / total
        attended = jnp.zeros((64, 384), f32)
        for n in range(4):
            attended = jnp.where(head_of_lane == n, mixed[64 * n : 64 * n + 64], attended)
        ATT[p, me] = attended.astype(bf)
        for k in (0, 1, 4, 5):
            amove(p, h, k).start()

    @pl.loop(0, 4)
    def _(g):
        for h in range(2):
            chunk(2 * g + h, h)

    def forward(t):
        wgot(t, 0)
        wmove(t, 2).start()
        wmove(t, 5).start()
        wgot(t, 1)
        wmove(t, 3).start()
        wmove(t, 6).start()

    def last(t):
        wgot(t, 2)
        wgot(t, 3)
        wmove(t, 7).start()

    def stage(moves):
        @pl.loop(0, 4)
        def _(g):
            for h in range(2):
                for waits, starts in moves:
                    for k in waits:
                        agot(2 * g + h, h, k)
                    for k in starts:
                        amove(2 * g + h, h, k).start()

    forward(0)
    stage([((0,), (2, 8, 9)), ((1,), (3, 12, 13))])
    forward(1)
    stage([((4,), (6,)), ((5,), (7,)), ((2, 3), (16, 17))])
    last(0)
    forward(2)
    stage([((8,), (10,)), ((9,), (11,)), ((12,), (14,)), ((13,), (15,))])
    stage([((16,), (18,)), ((17,), (19,))])
    last(1)
    for k in (4, 5, 6, 7):
        wgot(0, k)

    @pl.loop(0, 4)
    def _(g):
        for h in range(2):
            p = 2 * g + h
            for k in (6, 7, 10, 11, 14, 15, 18, 19):
                agot(p, h, k)
            PA[...] += lax.dot_general(
                WO[p], ATT[p].reshape(1024, 384), nt, preferred_element_type=f32
            )

    stream_ref[...] = PA[...].astype(bf)
    last(2)
    for t in (1, 2):
        for k in (4, 5, 6, 7):
            wgot(t, k)

    @pl.loop(1, 16)
    def _(d):
        j = (me + d) % 16
        block_copy(j).wait_send()
        gain_copy(j, me).wait_send()
        gain_copy(j, j).wait_recv()

    for t in range(3):
        for k in range(8):
            wmove(t, k).wait_send()

    @pl.loop(0, 4)
    def _(g):
        for h in range(2):
            for k in range(20):
                amove(2 * g + h, h, k).wait_send()

    own_gu.wait()
    own_dn.wait()


def attend_call(dealing, lengths, counts, parents, path, freq, gain, q, k, v, res, wo, gate, up, down, ck, cv):
    anyspace = pl.BlockSpec(memory_space=pl.ANY)
    vmem = pl.BlockSpec(memory_space=pltpu.VMEM)
    smem = pl.BlockSpec(memory_space=pltpu.SMEM)
    bf, f32 = jnp.bfloat16, jnp.float32
    dma = pltpu.SemaphoreType.DMA
    return pl.pallas_call(
        attend_kernel,
        out_shape=(
            jax.ShapeDtypeStruct((192, 1024), bf),
            jax.ShapeDtypeStruct((1, 8, 3072), bf),
            jax.ShapeDtypeStruct((1, 8, 3072), bf),
            jax.ShapeDtypeStruct((16, 1, 192), f32),
            jax.ShapeDtypeStruct((8, 1024, 384), bf),
            jax.ShapeDtypeStruct((8, 384, 512), bf),
        ),
        in_specs=[smem] * 3 + [vmem] * 12 + [anyspace] * 2,
        out_specs=(vmem, vmem, vmem, vmem, anyspace, anyspace),
        scratch_shapes=[
            pltpu.VMEM((8, 1536, 384), bf),
            pltpu.VMEM((8, 1536, 384), bf),
            pltpu.VMEM((16, 288, 128), bf),
            pltpu.VMEM((16, 288, 128), bf),
            pltpu.VMEM((8, 16, 64, 384), bf),
            pltpu.VMEM((192, 1024), f32),
            pltpu.VMEM((8, 192, 384), bf),
            pltpu.VMEM((1024, 384), bf),
            pltpu.VMEM((384, 512), bf),
            pltpu.VMEM((192, 192), bf),
            pltpu.VMEM((64, 192), f32),
            pltpu.VMEM((64, 192), f32),
            pltpu.VMEM((64, 64), f32),
            pltpu.VMEM((16, 64, 640), bf),
            pltpu.VMEM((16, 192, 64), bf),
            dma((2, 8)),
            dma((2,)),
            dma((16,)),
            dma((16,)),
            dma((16,)),
            dma((16,)),
            dma((3, 8)),
            dma((3, 8)),
            dma((8, 20)),
            dma((8, 20)),
        ],
        compiler_params=pltpu.CompilerParams(
            collective_id=1, has_side_effects=True, vmem_limit_bytes=60 * 1024 * 1024
        ),
        name="attend",
    )(dealing, lengths, counts, parents, path, freq, gain, q, k, v, res, wo, gate, up, down, ck, cv)


def mlp_kernel(
    dealt_ref, st_hbm, w_hbm, dn_hbm, gain_ref, out_ref,
    S, W, DN, acc, H, ss, T, R, Q, T2, R2, F, inverse,
    loc_sem, ag_send, ag_recv, rs_send, rs_recv, rt_send, rt_recv,
):
    me = lax.axis_index("col")
    z, x = me // 4, me % 4
    halves = (0, 1)
    a_own, b_own = (x, z), (z, x)

    def blk(h, a, b):
        return b * 4 + a if h == 0 else a * 4 + b

    def peer1(h, d):
        return blk(h, (a_own[h] + d + 4) % 4, b_own[h])

    def peer2(h, d):
        return blk(h, a_own[h], (b_own[h] + d + 4) % 4)

    stream_in = [
        pltpu.make_async_copy(st_hbm.at[:, pl.ds(512 * h, 512)], S.at[h, me], loc_sem.at[h])
        for h in halves
    ]
    w_in = pltpu.make_async_copy(w_hbm, W, loc_sem.at[2])
    dn_in = pltpu.make_async_copy(dn_hbm, DN, loc_sem.at[3])
    for c in stream_in:
        c.start()
    w_in.start()
    dn_in.start()

    barrier = pltpu.get_barrier_semaphore()
    for p in (peer1(0, 1), peer1(0, -1), peer1(1, 1), peer1(1, -1)):
        pl.semaphore_signal(barrier, inc=1, device_id={"col": p}, device_id_type=MESH)
    pl.semaphore_wait(barrier, 4)
    for c in stream_in:
        c.wait()

    sent = []

    def push(h, k, c, target, rows=None):
        ref = S.at[h, c] if rows is None else S.at[h, c, pl.ds(rows, 96)]
        cp = pltpu.make_async_remote_copy(
            src_ref=ref, dst_ref=ref, send_sem=ag_send.at[h, k], recv_sem=ag_recv.at[h, k],
            device_id={"col": target}, device_id_type=MESH,
        )
        cp.start()
        sent.append(cp)

    def arrived(h, k, c, rows=None):
        ref = S.at[h, c] if rows is None else S.at[h, c, pl.ds(rows, 96)]
        pltpu.make_async_remote_copy(
            src_ref=ref, dst_ref=ref, send_sem=ag_send.at[h, k], recv_sem=ag_recv.at[h, k],
            device_id={"col": me}, device_id_type=MESH,
        ).wait_recv()

    def at(h, da, db):
        return blk(h, (a_own[h] + da + 4) % 4, (b_own[h] + db + 4) % 4)

    offs = (0, -1, 1, 2)
    for h in halves:
        push(h, 0, me, peer1(h, 1))
        push(h, 1, me, peer1(h, -1))
    for h in halves:
        push(h, 4, me, peer2(h, 1))
        push(h, 5, me, peer2(h, -1))

    acc[...] = jnp.zeros_like(acc)
    ss[...] = jnp.zeros_like(ss)
    for h in halves:
        arrived(h, 0, at(h, -1, 0))
        push(h, 2, at(h, -1, 0), peer1(h, 1), 0)
        push(h, 8, at(h, -1, 0), peer2(h, 1))
        push(h, 9, at(h, -1, 0), peer2(h, -1))
        arrived(h, 1, at(h, 1, 0))
        push(h, 3, at(h, 1, 0), peer1(h, -1), 96)
        push(h, 12, at(h, 1, 0), peer2(h, 1))
        push(h, 13, at(h, 1, 0), peer2(h, -1))

    def second(j):
        for h in halves:
            base = 4 + 4 * j
            arrived(h, base, at(h, offs[j], -1))
            push(h, base + 2, at(h, offs[j], -1), peer2(h, 1), 0)
            arrived(h, base + 1, at(h, offs[j], 1))
            push(h, base + 3, at(h, offs[j], 1), peer2(h, -1), 96)

    def square(h, c):
        v = S[h, c].astype(jnp.float32)
        ss[h] += jnp.sum(v * v, axis=0, keepdims=True)

    def fold_a(zz):
        for i in range(4):
            square(0, zz * 4 + i)
        k0 = S[0, pl.ds(zz * 4, 2)].reshape(384, 512)
        k1 = S[0, pl.ds(zz * 4 + 2, 2)].reshape(384, 512)

        @pl.loop(0, 4)
        def _(m):
            rows = pl.ds(pl.multiple_of(m * 256, 256), 256)
            acc[0, rows] += jnp.dot(
                W[2 * zz, rows], k0, preferred_element_type=jnp.float32
            ) + jnp.dot(W[2 * zz + 1, rows], k1, preferred_element_type=jnp.float32)

    def fold_b(q):
        @pl.loop(0, 2)
        def _(g):
            for i in range(2):
                for e in range(2):
                    square(1, (2 * g + i) * 4 + 2 * q + e)
            k0 = S[1, pl.ds(8 * g + 2 * q, 2)].reshape(384, 512)
            k1 = S[1, pl.ds(8 * g + 4 + 2 * q, 2)].reshape(384, 512)

            @pl.loop(0, 4)
            def _(m):
                rows = pl.ds(pl.multiple_of(m * 256, 256), 256)
                acc[1, rows] += jnp.dot(
                    W[4 * g + q, rows], k0, preferred_element_type=jnp.float32
                ) + jnp.dot(W[4 * g + 2 + q, rows], k1, preferred_element_type=jnp.float32)

    second(0)
    for h in halves:
        arrived(h, 2, at(h, 2, 0), 0)
        arrived(h, 3, at(h, 2, 0), 96)
        push(h, 16, at(h, 2, 0), peer2(h, 1))
        push(h, 17, at(h, 2, 0), peer2(h, -1))
    w_in.wait()

    @pl.loop(0, 8)
    def _(r):
        both = jnp.concatenate([gain_ref[2 * r], gain_ref[2 * r + 1]], axis=1)
        W[r] = W[r] * both.astype(jnp.bfloat16)

    @pl.loop(0, 16)
    def _(i):
        slot = jnp.int32(0)
        for j in range(16):
            slot = jnp.where(dealt_ref[0, j] == i, j, slot)
        inverse[i] = slot

    fold_a(z)
    second(1)
    second(2)
    second(3)

    @pl.loop(0, 2)
    def _(i):
        fold_a((z + 3 + 2 * i) % 4)

    fold_b(x // 2)
    for h in halves:
        for j in range(4):
            arrived(h, 6 + 4 * j, at(h, offs[j], 2), 0)
            arrived(h, 7 + 4 * j, at(h, offs[j], 2), 96)
    fold_a((z + 2) % 4)
    fold_b(1 - x // 2)
    for cp in sent:
        cp.wait_send()

    for h in halves:
        factor = lax.rsqrt(ss[h] * (1.0 / D) + 1e-05)

        @pl.loop(0, 4)
        def _(m, h=h, factor=factor):
            rows = pl.ds(pl.multiple_of(m * 128, 128), 128)
            uprows = pl.ds(pl.multiple_of(512 + m * 128, 128), 128)
            g = acc[h, rows] * factor
            u = acc[h, uprows] * factor
            H[h, rows] = (g / (1.0 + jnp.exp(-g)) * u).astype(jnp.bfloat16)

    dn_in.wait()

    def part(h, c):
        rows = pl.ds(pl.multiple_of(c * 192, 192), 192)
        return jnp.dot(DN[rows], H[h], preferred_element_type=jnp.float32)

    sent = []

    def send1(h, kind, i):
        d = 1 if kind % 2 == 0 else -1
        cp = pltpu.make_async_remote_copy(
            src_ref=T.at[h, kind, i], dst_ref=R.at[h, kind, i],
            send_sem=rs_send.at[h, kind, i], recv_sem=rs_recv.at[h, kind, i],
            device_id={"col": peer1(h, d)}, device_id_type=MESH,
        )
        cp.start()
        sent.append(cp)

    def got1(h, kind, i):
        pltpu.make_async_remote_copy(
            src_ref=T.at[h, kind, i], dst_ref=R.at[h, kind, i],
            send_sem=rs_send.at[h, kind, i], recv_sem=rs_recv.at[h, kind, i],
            device_id={"col": me}, device_id_type=MESH,
        ).wait_recv()

    def dest(h, da, b):
        return blk(h, (a_own[h] + da + 4) % 4, b)

    for kind, da, b0 in ((0, 2, 0), (1, 2, 2), (4, 1, 2), (5, -1, 0)):
        for i in range(2):
            for h in halves:
                T[h, kind, i] = part(h, dest(h, da, b0 + i)).astype(jnp.bfloat16)
                send1(h, kind, i)
    for kind, da, b0 in ((2, 1, 0), (3, -1, 2)):
        for i in range(2):
            for h in halves:
                mine = part(h, dest(h, da, b0 + i))
                got1(h, kind - 2, i)
                T[h, kind, i] = (mine + R[h, kind - 2, i].astype(jnp.float32)).astype(jnp.bfloat16)
                send1(h, kind, i)
    for b in range(4):
        for h in halves:
            mine = part(h, dest(h, 0, b))
            s_kind, d_kind = (2, 5) if b < 2 else (3, 4)
            got1(h, s_kind, b % 2)
            got1(h, d_kind, b % 2)
            Q[h, b] = (
                mine
                + R[h, s_kind, b % 2].astype(jnp.float32)
                + R[h, d_kind, b % 2].astype(jnp.float32)
            ).astype(jnp.bfloat16)
    def copy2(h, kind, src, target):
        return pltpu.make_async_remote_copy(
            src_ref=src, dst_ref=R2.at[h, kind],
            send_sem=rt_send.at[h, kind], recv_sem=rt_recv.at[h, kind],
            device_id={"col": target}, device_id_type=MESH,
        )

    def bmod(h, d):
        return (b_own[h] + d + 4) % 4

    for h in halves:
        for kind, d, row in ((0, 2, 0), (1, 2, 96), (4, 1, 96), (5, -1, 0)):
            cp = copy2(h, kind, Q.at[h, bmod(h, d), pl.ds(row, 96)], peer2(h, 1 if kind % 2 == 0 else -1))
            cp.start()
            sent.append(cp)
    for h in halves:
        for kind, d, row in ((2, 1, 0), (3, -1, 96)):
            copy2(h, kind - 2, T2.at[h, 0], me).wait_recv()
            T2[h, kind - 2] = (
                Q[h, bmod(h, d), pl.ds(row, 96)].astype(jnp.float32)
                + R2[h, kind - 2].astype(jnp.float32)
            ).astype(jnp.bfloat16)
            cp = copy2(h, kind, T2.at[h, kind - 2], peer2(h, 1 if kind == 2 else -1))
            cp.start()
            sent.append(cp)
    for h in halves:
        for row, s_kind, d_kind in ((0, 2, 5), (96, 3, 4)):
            copy2(h, s_kind, T2.at[h, 0], me).wait_recv()
            copy2(h, d_kind, T2.at[h, 0], me).wait_recv()
            rows = (
                S[h, me, pl.ds(row, 96)].astype(jnp.float32)
                + Q[h, b_own[h], pl.ds(row, 96)].astype(jnp.float32)
                + R2[h, s_kind].astype(jnp.float32)
                + R2[h, d_kind].astype(jnp.float32)
            ).astype(jnp.bfloat16)
            for n in range(8):
                F[8 * h + n, pl.ds(row, 96)] = rows[:, 64 * n : 64 * n + 64]

    @pl.loop(0, 8)
    def _(m):
        out_ref[:, pl.ds(pl.multiple_of(m * 128, 128), 128)] = jnp.concatenate(
            [F[inverse[2 * m]], F[inverse[2 * m + 1]]], axis=1
        )

    for cp in sent:
        cp.wait_send()


def mlp_call(dealing, stream_t, weights, down_t, gain):
    anyspace = pl.BlockSpec(memory_space=pl.ANY)
    vmem = pl.BlockSpec(memory_space=pltpu.VMEM)
    bf, f32 = jnp.bfloat16, jnp.float32
    dma = pltpu.SemaphoreType.DMA
    return pl.pallas_call(
        mlp_kernel,
        out_shape=jax.ShapeDtypeStruct((192, 1024), bf),
        in_specs=[pl.BlockSpec(memory_space=pltpu.SMEM), anyspace, anyspace, anyspace, vmem],
        out_specs=vmem,
        scratch_shapes=[
            pltpu.VMEM((2, 16, 192, 512), bf),
            pltpu.VMEM((8, 1024, 384), bf),
            pltpu.VMEM((3072, 512), bf),
            pltpu.VMEM((2, 1024, 512), f32),
            pltpu.VMEM((2, 512, 512), bf),
            pltpu.VMEM((2, 1, 512), f32),
            pltpu.VMEM((2, 6, 2, 192, 512), bf),
            pltpu.VMEM((2, 6, 2, 192, 512), bf),
            pltpu.VMEM((2, 4, 192, 512), bf),
            pltpu.VMEM((2, 2, 96, 512), bf),
            pltpu.VMEM((2, 6, 96, 512), bf),
            pltpu.VMEM((16, 192, 64), bf),
            pltpu.SMEM((16,), jnp.int32),
            dma((4,)),
            dma((2, 20)),
            dma((2, 20)),
            dma((2, 6, 2)),
            dma((2, 6, 2)),
            dma((2, 6)),
            dma((2, 6)),
        ],
        compiler_params=pltpu.CompilerParams(
            collective_id=0, has_side_effects=True, vmem_limit_bytes=60 * 1024 * 1024
        ),
        name="mlp",
    )(dealing, stream_t, weights, down_t, gain)


def body(
    dealing,
    residual,
    queries,
    draft_keys,
    draft_values,
    cache_keys,
    cache_values,
    cache_lengths,
    parents,
    draft_counts,
    accepted,
    out_weight,
    norm_gain,
    gate_weight,
    up_weight,
    down_weight,
):
    freq = np.power(10000.0, -(np.arange(192) % 48) * (2.0 / HEAD_DIM)).astype(np.float32)

    stream_t, new_keys, new_values, gains, gate_up, down_t = attend_call(
        dealing,
        cache_lengths,
        draft_counts,
        parents,
        accepted,
        jnp.asarray(freq).reshape(1, 192),
        norm_gain,
        queries.T,
        draft_keys.T,
        draft_values.T,
        residual.T,
        out_weight.T,
        gate_weight,
        up_weight,
        down_weight,
        cache_keys,
        cache_values,
    )
    out_t = mlp_call(dealing, stream_t, gate_up, down_t.reshape(3072, 512), gains)
    return (out_t.T, new_keys, new_values)


def solution(mesh):
    placed = (
        P("row", None),
        P("row", "col"),
        P("row", "col"),
        P("row", "col"),
        P("row", "col"),
        P(("row", "col"), None, None),
        P(("row", "col"), None, None),
        P(("row", "col")),
        P(("row", "col"), None),
        P(("row", "col")),
        P(("row", "col"), None),
        P("row", "col"),
        P("col"),
        P("row", "col"),
        P("row", "col"),
        P("col", "row"),
    )
    return jax.shard_map(
        body,
        mesh=mesh,
        in_specs=placed,
        out_specs=(P("row", "col"), P(("row", "col"), None, None), P(("row", "col"), None, None)),
        check_vma=False,
    )
```

```python
import math

import jax
import jax.numpy as jnp
import numpy as np
from jax import lax
from jax.experimental import pallas as pl
from jax.experimental.pallas import tpu as pltpu
from jax.sharding import PartitionSpec as P

D = 3072
HEAD_DIM = 96
MESH = pl.DeviceIdType.MESH

OFFS = (0, -1, 1, 2)
HOPS = [
    ((0, 0), 1, 1, None, (-1, 0)),
    ((0, 0), 1, -1, None, (1, 0)),
    ((-1, 0), 1, 1, 0, (2, 0)),
    ((1, 0), 1, -1, 1, (2, 0)),
]
for _d in OFFS:
    HOPS += [
        ((_d, 0), 2, 1, None, (_d, -1)),
        ((_d, 0), 2, -1, None, (_d, 1)),
        ((_d, -1), 2, 1, 0, (_d, 2)),
        ((_d, 1), 2, -1, 1, (_d, 2)),
    ]


def attend_kernel(
    dealt_ref, length_ref, count_ref, parent_ref, path_ref, freq_ref, gain_ref,
    q_ref, k_ref, v_ref, res_ref, wo_ref, gate_ref, up_ref, down_ref, ck_hbm, cv_hbm,
    stream_ref, nk_ref, nv_ref, gains_ref, gu_out, dn_out,
    KC, VC, SB, RB, ATT, PA, WO, TG, TD, turn, cosine, sine, anc_ref, TT, RB1,
    kv_sem, loc_sem, x_send, x_recv, n_send, n_recv, w_send, w_recv, a_send, a_recv,
):
    f32, bf = jnp.float32, jnp.bfloat16
    row = lax.axis_index("row")
    me = lax.axis_index("col")
    z, x = me // 4, me % 4
    y, core = row // 2, row % 2

    def near(g):
        return g + g // 2 - 2 * (g // 3)

    def heads_at(i, zz):
        return 2 * ((zz + near(i // 2)) % 4) + i % 2

    def cache_in(i):
        lanes = pl.ds(pl.multiple_of(heads_at(i, z) * 384, 128), 384)
        return (
            pltpu.make_async_copy(ck_hbm.at[0, :, lanes], KC.at[i], kv_sem.at[0, i]),
            pltpu.make_async_copy(cv_hbm.at[0, :, lanes], VC.at[i], kv_sem.at[1, i]),
        )

    @pl.loop(0, 8)
    def _(p):
        for c in cache_in(p):
            c.start()

    barrier = pltpu.get_barrier_semaphore()

    @pl.loop(1, 16)
    def _(d):
        pl.semaphore_signal(
            barrier, inc=1, device_id={"col": (me + d) % 16}, device_id_type=MESH
        )

    row_up = ((y + 1) % 4) * 2 + core
    row_down = ((y + 3) % 4) * 2 + core
    row_twin = y * 2 + 1 - core
    for r in (row_up, row_down, row_twin):
        pl.semaphore_signal(barrier, inc=1, device_id={"row": r}, device_id_type=MESH)

    for n, ref in enumerate((q_ref, k_ref, v_ref)):
        for m in range(4):
            rows = ref[:, 256 * m : 256 * m + 256].astype(f32).T.astype(bf)
            TT[4 * m : 4 * m + 4, :, 192 * n : 192 * n + 192] = rows.reshape(4, 64, 192)

    @pl.loop(0, 16)
    def _(j):
        block = TT[dealt_ref[0, j]]
        for n in range(4):
            SB[j, 64 * n : 64 * n + 64] = block[:, 128 * n : 128 * n + 128]
        SB[j, 256:288] = jnp.concatenate([block[0:32, 512:576], block[32:64, 512:576]], axis=1)

    gains_ref[me] = gain_ref[...].astype(f32).reshape(1, 192)
    pl.semaphore_wait(barrier, 18)

    def block_copy(j):
        return pltpu.make_async_remote_copy(
            src_ref=SB.at[j], dst_ref=RB.at[me], send_sem=x_send.at[j], recv_sem=x_recv.at[me],
            device_id={"col": j}, device_id_type=MESH,
        )

    def block_arrival(s):
        return pltpu.make_async_remote_copy(
            src_ref=SB.at[s], dst_ref=RB.at[s], send_sem=x_send.at[s], recv_sem=x_recv.at[s],
            device_id={"col": s}, device_id_type=MESH,
        )

    def gain_copy(j, slot):
        return pltpu.make_async_remote_copy(
            src_ref=gains_ref.at[me], dst_ref=gains_ref.at[slot],
            send_sem=n_send.at[j], recv_sem=n_recv.at[slot],
            device_id={"col": j}, device_id_type=MESH,
        )

    RB[me] = SB[me]

    @pl.loop(1, 16)
    def _(d):
        j = ((z + 4 - near(d // 4)) % 4) * 4 + (x + near(d % 4)) % 4
        block_copy(j).start()

    @pl.loop(1, 16)
    def _(d):
        gain_copy((me + d) % 16, me).start()

    WO[row] = wo_ref[...]
    TG[0:512] = gate_ref[...].astype(f32).T.astype(bf)
    TG[512:1024] = up_ref[...].astype(f32).T.astype(bf)
    TD[...] = down_ref[...].astype(f32).T.astype(bf)
    own_gu = pltpu.make_async_copy(TG, gu_out.at[row], loc_sem.at[0])
    own_dn = pltpu.make_async_copy(TD, dn_out.at[row], loc_sem.at[1])
    own_gu.start()
    own_dn.start()
    tables = ((WO, None, 192), (gu_out, TG, 1024), (dn_out, TD, 384))
    yb = {
        0: row, -1: row_down, 1: row_up, 2: ((y + 2) % 4) * 2 + core,
    }
    wmoves = [
        (0, None, row_up, -1, False),
        (0, None, row_down, 1, False),
        (-1, 0, row_up, 2, False),
        (1, 1, row_down, 2, False),
        (0, None, row_twin, 0, True),
        (-1, None, row_twin, -1, True),
        (1, None, row_twin, 1, True),
        (2, None, row_twin, 2, True),
    ]

    def wref(t, index, part, own):
        table, mine, size = tables[t]
        if own and mine is not None:
            return mine
        if part is None:
            return table.at[index]
        return table.at[index, pl.ds(part * (size // 2), size // 2)]

    def wmove(t, k):
        d, part, target, _, _ = wmoves[k]
        return pltpu.make_async_remote_copy(
            src_ref=wref(t, yb[d], part, d == 0), dst_ref=wref(t, yb[d], part, False),
            send_sem=w_send.at[t, k], recv_sem=w_recv.at[t, k],
            device_id={"row": target}, device_id_type=MESH,
        )

    def wgot(t, k):
        _, part, target, d, twin = wmoves[k]
        index = yb[d] + 1 - 2 * core if twin else yb[d]
        ref = wref(t, index, part, False)
        pltpu.make_async_remote_copy(
            src_ref=ref, dst_ref=ref, send_sem=w_send.at[t, k], recv_sem=w_recv.at[t, k],
            device_id={"row": target}, device_id_type=MESH,
        ).wait_recv()

    for t in range(3):
        for k in (0, 1, 4):
            wmove(t, k).start()

    i64 = lax.broadcasted_iota(jnp.int32, (64, 64), 0)
    j64 = lax.broadcasted_iota(jnp.int32, (64, 64), 1)
    anc = jnp.logical_or(parent_ref[...] == i64, i64 == j64).astype(f32)
    for sweep in range(6):
        half = anc.astype(bf)
        anc = jnp.minimum(jnp.dot(half, half, preferred_element_type=f32), 1.0)
    anc = anc.T
    length = length_ref[0]
    live = count_ref[0]
    position = length.astype(f32) + jnp.sum(anc, axis=1, keepdims=True) - 1.0
    angle = position * freq_ref[...]
    cosine[...] = jnp.cos(angle)
    sine[...] = jnp.sin(angle)
    anc_ref[...] = jnp.where(j64 < live, anc, 0.0)
    ti = lax.broadcasted_iota(jnp.int32, (192, 192), 0)
    tj = lax.broadcasted_iota(jnp.int32, (192, 192), 1)
    low = (tj % 96) < 48
    turn[...] = jnp.where(
        jnp.logical_and(low, ti == tj + 48), -1.0,
        jnp.where(jnp.logical_and(jnp.logical_not(low), ti == tj - 48), 1.0, 0.0),
    ).astype(bf)

    for j in range(16):
        RB1[j] = res_ref[:, 64 * j : 64 * j + 64]

    @pl.loop(0, 8)
    def _(m):
        pair = jnp.concatenate([RB1[dealt_ref[0, 2 * m]], RB1[dealt_ref[0, 2 * m + 1]]], axis=1)
        PA[:, pl.ds(pl.multiple_of(m * 128, 128), 128)] = pair.astype(f32)

    def rotated(rows):
        swapped = jnp.dot(rows, turn[...], preferred_element_type=f32)
        return (rows.astype(f32) * cosine[...] + swapped * sine[...]).astype(bf)

    a_own, b_own = (x, z), (z, x)

    def at(h, da, db):
        a, b = (a_own[h] + da + 4) % 4, (b_own[h] + db + 4) % 4
        return b * 4 + a if h == 0 else a * 4 + b

    def piece(p, c, part):
        return ATT.at[p, c] if part is None else ATT.at[p, c, pl.ds(32 * part, 32)]

    def amove(p, h, k):
        (da, db), axis, way, part, _ = HOPS[k]
        ref = piece(p, at(h, da, db), part)
        target = at(h, way, 0) if axis == 1 else at(h, 0, way)
        return pltpu.make_async_remote_copy(
            src_ref=ref, dst_ref=ref, send_sem=a_send.at[p, k], recv_sem=a_recv.at[p, k],
            device_id={"col": target}, device_id_type=MESH,
        )

    def agot(p, h, k):
        _, axis, way, part, (da, db) = HOPS[k]
        ref = piece(p, at(h, da, db), part)
        target = at(h, way, 0) if axis == 1 else at(h, 0, way)
        pltpu.make_async_remote_copy(
            src_ref=ref, dst_ref=ref, send_sem=a_send.at[p, k], recv_sem=a_recv.at[p, k],
            device_id={"col": target}, device_id_type=MESH,
        ).wait_recv()

    nt = (((1,), (1,)), ((), ()))
    scale = 1.0 / math.sqrt(HEAD_DIM)
    head_of_lane = lax.broadcasted_iota(jnp.int32, (64, 384), 1) // 96
    key_live = lax.broadcasted_iota(jnp.int32, (1, 1536), 1) < length
    path_hot = (
        (path_ref[...] == lax.broadcasted_iota(jnp.int32, (64, 8), 0)).astype(f32).T.astype(bf)
    )

    def chunk(i, h):
        p = heads_at(i, z)
        for e in range(2):
            @pl.when(2 * p + e != me)
            def _(e=e):
                block_arrival(2 * p + e).wait_recv()
        def unpack(s):
            block = RB[s]
            tail = jnp.concatenate([block[256:288, 0:64], block[256:288, 64:128]], axis=0)
            return jnp.concatenate([block[64 * n : 64 * n + 64] for n in range(4)] + [tail], axis=1)

        first, other = unpack(2 * p), unpack(2 * p + 1)
        q = jnp.concatenate([rotated(first[:, 0:192]), rotated(other[:, 0:192])], axis=1)
        kd = jnp.concatenate([rotated(first[:, 192:384]), rotated(other[:, 192:384])], axis=1)
        vd = jnp.concatenate([first[:, 384:576], other[:, 384:576]], axis=1)
        lanes = pl.ds(pl.multiple_of(p * 384, 128), 384)
        nk_ref[0, :, lanes] = jnp.dot(path_hot, kd, preferred_element_type=f32).astype(bf)
        nv_ref[0, :, lanes] = jnp.dot(path_hot, vd, preferred_element_type=f32).astype(bf)
        wide = jnp.concatenate(
            [jnp.where(head_of_lane == n, q, jnp.zeros_like(q)) for n in range(4)], axis=0
        )
        for c in cache_in(i):
            c.wait()
        old = lax.dot_general(wide, KC[i], nt, preferred_element_type=f32)
        old = jnp.where(key_live, old, -jnp.inf)
        new = lax.dot_general(wide, kd, nt, preferred_element_type=f32)
        allowed = jnp.concatenate([anc_ref[...]] * 4, axis=0) > 0.5
        new = jnp.where(allowed, new, -jnp.inf)
        top = jnp.maximum(
            jnp.max(old, axis=1, keepdims=True), jnp.max(new, axis=1, keepdims=True)
        )
        w_old = jnp.exp((old - top) * scale)
        w_new = jnp.exp((new - top) * scale)
        total = jnp.sum(w_old, axis=1, keepdims=True) + jnp.sum(w_new, axis=1, keepdims=True)
        mixed = jnp.dot(w_old.astype(bf), VC[i], preferred_element_type=f32) + jnp.dot(
            w_new.astype(bf), vd, preferred_element_type=f32
        )
        mixed = mixed / total
        attended = jnp.zeros((64, 384), f32)
        for n in range(4):
            attended = jnp.where(head_of_lane == n, mixed[64 * n : 64 * n + 64], attended)
        ATT[i, me] = attended.astype(bf)
        for k in (0, 1, 4, 5):
            amove(i, h, k).start()

    @pl.loop(0, 4)
    def _(g):
        for h in range(2):
            chunk(2 * g + h, h)

    def forward(t):
        wgot(t, 0)
        wmove(t, 2).start()
        wmove(t, 5).start()
        wgot(t, 1)
        wmove(t, 3).start()
        wmove(t, 6).start()

    def last(t):
        wgot(t, 2)
        wgot(t, 3)
        wmove(t, 7).start()

    def stage(moves):
        @pl.loop(0, 4)
        def _(g):
            for h in range(2):
                for waits, starts in moves:
                    for k in waits:
                        agot(2 * g + h, h, k)
                    for k in starts:
                        amove(2 * g + h, h, k).start()

    forward(0)
    stage([((0,), (2, 8, 9)), ((1,), (3, 12, 13))])
    forward(1)
    stage([((4,), (6,)), ((5,), (7,)), ((2, 3), (16, 17))])
    last(0)
    forward(2)
    stage([((8,), (10,)), ((9,), (11,)), ((12,), (14,)), ((13,), (15,))])
    stage([((16,), (18,)), ((17,), (19,))])
    last(1)
    for k in (4, 5, 6, 7):
        wgot(0, k)

    @pl.loop(0, 4)
    def _(g):
        for h in range(2):
            p = 2 * g + h
            for k in (6, 7, 10, 11, 14, 15, 18, 19):
                agot(p, h, k)
            for zz in range(4):
                PA[:, 256 * zz : 256 * zz + 256] += lax.dot_general(
                    WO[heads_at(p, zz)], ATT[p, 4 * zz : 4 * zz + 4].reshape(256, 384), nt,
                    preferred_element_type=f32,
                )

    stream_ref[...] = PA[...].astype(bf)
    last(2)
    for t in (1, 2):
        for k in (4, 5, 6, 7):
            wgot(t, k)

    @pl.loop(1, 16)
    def _(d):
        j = (me + d) % 16
        block_copy(j).wait_send()
        gain_copy(j, me).wait_send()
        gain_copy(j, j).wait_recv()

    for t in range(3):
        for k in range(8):
            wmove(t, k).wait_send()

    @pl.loop(0, 4)
    def _(g):
        for h in range(2):
            for k in range(20):
                amove(2 * g + h, h, k).wait_send()

    own_gu.wait()
    own_dn.wait()


def attend_call(dealing, lengths, counts, parents, path, freq, gain, q, k, v, res, wo, gate, up, down, ck, cv):
    anyspace = pl.BlockSpec(memory_space=pl.ANY)
    vmem = pl.BlockSpec(memory_space=pltpu.VMEM)
    smem = pl.BlockSpec(memory_space=pltpu.SMEM)
    bf, f32 = jnp.bfloat16, jnp.float32
    dma = pltpu.SemaphoreType.DMA
    return pl.pallas_call(
        attend_kernel,
        out_shape=(
            jax.ShapeDtypeStruct((192, 1024), bf),
            jax.ShapeDtypeStruct((1, 8, 3072), bf),
            jax.ShapeDtypeStruct((1, 8, 3072), bf),
            jax.ShapeDtypeStruct((16, 1, 192), f32),
            jax.ShapeDtypeStruct((8, 1024, 384), bf),
            jax.ShapeDtypeStruct((8, 384, 512), bf),
        ),
        in_specs=[smem] * 3 + [vmem] * 12 + [anyspace] * 2,
        out_specs=(vmem, vmem, vmem, vmem, anyspace, anyspace),
        scratch_shapes=[
            pltpu.VMEM((8, 1536, 384), bf),
            pltpu.VMEM((8, 1536, 384), bf),
            pltpu.VMEM((16, 288, 128), bf),
            pltpu.VMEM((16, 288, 128), bf),
            pltpu.VMEM((8, 16, 64, 384), bf),
            pltpu.VMEM((192, 1024), f32),
            pltpu.VMEM((8, 192, 384), bf),
            pltpu.VMEM((1024, 384), bf),
            pltpu.VMEM((384, 512), bf),
            pltpu.VMEM((192, 192), bf),
            pltpu.VMEM((64, 192), f32),
            pltpu.VMEM((64, 192), f32),
            pltpu.VMEM((64, 64), f32),
            pltpu.VMEM((16, 64, 640), bf),
            pltpu.VMEM((16, 192, 64), bf),
            dma((2, 8)),
            dma((2,)),
            dma((16,)),
            dma((16,)),
            dma((16,)),
            dma((16,)),
            dma((3, 8)),
            dma((3, 8)),
            dma((8, 20)),
            dma((8, 20)),
        ],
        compiler_params=pltpu.CompilerParams(
            collective_id=1, has_side_effects=True, vmem_limit_bytes=60 * 1024 * 1024
        ),
        name="attend",
    )(dealing, lengths, counts, parents, path, freq, gain, q, k, v, res, wo, gate, up, down, ck, cv)


def mlp_kernel(
    dealt_ref, st_hbm, w_hbm, dn_hbm, gain_ref, out_ref,
    S, W, DN, acc, H, ss, T, R, Q, T2, R2, F, inverse,
    st_sem, w_sem, ag_send, ag_recv, rs_send, rs_recv, rt_send, rt_recv,
):
    f32, bf = jnp.float32, jnp.bfloat16
    me = lax.axis_index("col")
    z, x = me // 4, me % 4
    halves = (0, 1)
    a_own, b_own = (x, z), (z, x)

    def blk(h, a, b):
        return b * 4 + a if h == 0 else a * 4 + b

    def at(h, da, db):
        return blk(h, (a_own[h] + da + 4) % 4, (b_own[h] + db + 4) % 4)

    def peer(h, axis, way):
        return at(h, way, 0) if axis == 1 else at(h, 0, way)

    stream_in = [
        pltpu.make_async_copy(
            st_hbm.at[:, pl.ds(512 * t + 256 * h, 256)], S.at[t, h, me], st_sem.at[t, h]
        )
        for t in range(2)
        for h in halves
    ]
    w_in = [
        pltpu.make_async_copy(
            w_hbm.at[r], W.at[r // 2, :, pl.ds(384 * (r % 2), 384)], w_sem.at[r]
        )
        for r in range(8)
    ]
    dn_in = pltpu.make_async_copy(dn_hbm, DN, w_sem.at[8])
    for c in stream_in + w_in + [dn_in]:
        c.start()

    barrier = pltpu.get_barrier_semaphore()
    for p in (peer(0, 1, 1), peer(0, 1, -1), peer(0, 2, 1), peer(0, 2, -1)):
        pl.semaphore_signal(barrier, inc=1, device_id={"col": p}, device_id_type=MESH)
    pl.semaphore_wait(barrier, 4)
    for c in stream_in:
        c.wait()

    sent = []

    def gmove(t, h, k, offset):
        (da, db), axis, way, part, landed = HOPS[k]
        if offset == "landed":
            da, db = landed
        ref = S.at[t, h, at(h, da, db)]
        if part is not None:
            ref = S.at[t, h, at(h, da, db), pl.ds(96 * part, 96)]
        return pltpu.make_async_remote_copy(
            src_ref=ref, dst_ref=ref, send_sem=ag_send.at[t, h, k], recv_sem=ag_recv.at[t, h, k],
            device_id={"col": peer(h, axis, way)}, device_id_type=MESH,
        )

    def push(t, h, *ks):
        for k in ks:
            cp = gmove(t, h, k, "sent")
            cp.start()
            sent.append(cp)

    def got(t, h, *ks):
        for k in ks:
            gmove(t, h, k, "landed").wait_recv()

    def gather0(t):
        for h in halves:
            push(t, h, 0, 1)
        for h in halves:
            push(t, h, 4, 5)

    def gather1(t):
        for h in halves:
            got(t, h, 0)
            push(t, h, 2, 8, 9)
            got(t, h, 1)
            push(t, h, 3, 12, 13)

    def gather2(t):
        for h in halves:
            for k in (4, 5):
                got(t, h, k)
                push(t, h, k + 2)
            got(t, h, 2, 3)
            push(t, h, 16, 17)

    def gather3(t):
        for h in halves:
            for k in (8, 9, 12, 13):
                got(t, h, k)
                push(t, h, k + 2)

    def gather4(t):
        for h in halves:
            for k in (16, 17):
                got(t, h, k)
                push(t, h, k + 2)

    def gather5(t):
        for h in halves:
            got(t, h, 6, 7, 10, 11, 14, 15, 18, 19)

    def squares(t, h, v):
        v = v.astype(f32)
        ss[t, h] += jnp.sum(v * v, axis=0, keepdims=True)

    def fold_a(t, zz):
        k = S[t, 0, pl.ds(zz * 4, 4)].reshape(768, 256)
        squares(t, 0, k)

        @pl.loop(0, 4)
        def _(m):
            rows = pl.ds(pl.multiple_of(m * 256, 256), 256)
            acc[t, 0, rows] += jnp.dot(W[zz, rows], k, preferred_element_type=f32)

    def fold_b(t, q):
        lanes = pl.ds(pl.multiple_of(q * 384, 128), 384)

        @pl.loop(0, 4)
        def _(g):
            k = S[t, 1, pl.ds(4 * g + 2 * q, 2)].reshape(384, 256)
            squares(t, 1, k)

            @pl.loop(0, 4)
            def _(m):
                rows = pl.ds(pl.multiple_of(m * 256, 256), 256)
                acc[t, 1, rows] += jnp.dot(W[g, rows, lanes], k, preferred_element_type=f32)

    def activate(t):
        for h in halves:
            factor = lax.rsqrt(ss[t, h] * (1.0 / D) + 1e-05)

            @pl.loop(0, 4)
            def _(m, h=h, factor=factor):
                rows = pl.ds(pl.multiple_of(m * 128, 128), 128)
                uprows = pl.ds(pl.multiple_of(512 + m * 128, 128), 128)
                g = acc[t, h, rows] * factor
                u = acc[t, h, uprows] * factor
                H[t, h, rows] = (g / (1.0 + jnp.exp(-g)) * u).astype(bf)

    def parts(t, h, da, b0):
        rows = []
        for b in (b0, b0 + 1):
            c = blk(h, (a_own[h] + da + 4) % 4, b)
            rows.append(DN[pl.ds(pl.multiple_of(c * 192, 192), 192)])
        return jnp.dot(
            jnp.concatenate(rows, axis=0), H[t, h], preferred_element_type=f32
        ).reshape(2, 192, 256)

    def smove(t, h, kind):
        return pltpu.make_async_remote_copy(
            src_ref=T.at[t, h, kind], dst_ref=R.at[t, h, kind],
            send_sem=rs_send.at[t, h, kind], recv_sem=rs_recv.at[t, h, kind],
            device_id={"col": peer(h, 1, 1 if kind % 2 == 0 else -1)}, device_id_type=MESH,
        )

    def sum1(t):
        for kind, da, b0 in ((0, 2, 0), (1, 2, 2), (4, 1, 2), (5, -1, 0)):
            for h in halves:
                T[t, h, kind] = parts(t, h, da, b0).astype(bf)
                cp = smove(t, h, kind)
                cp.start()
                sent.append(cp)

    def sum2(t):
        for kind, da, b0 in ((2, 1, 0), (3, -1, 2)):
            for h in halves:
                mine = parts(t, h, da, b0)
                smove(t, h, kind - 2).wait_recv()
                T[t, h, kind] = (mine + R[t, h, kind - 2].astype(f32)).astype(bf)
                cp = smove(t, h, kind)
                cp.start()
                sent.append(cp)

    def bmod(h, d):
        return (b_own[h] + d + 4) % 4

    def qmove(t, h, kind, src):
        return pltpu.make_async_remote_copy(
            src_ref=src, dst_ref=R2.at[t, h, kind],
            send_sem=rt_send.at[t, h, kind], recv_sem=rt_recv.at[t, h, kind],
            device_id={"col": peer(h, 2, 1 if kind % 2 == 0 else -1)}, device_id_type=MESH,
        )

    def sum3(t):
        for b0, s_kind, d_kind in ((0, 2, 5), (2, 3, 4)):
            for h in halves:
                mine = parts(t, h, 0, b0)
                smove(t, h, s_kind).wait_recv()
                smove(t, h, d_kind).wait_recv()
                Q[t, h, b0 : b0 + 2] = (
                    mine + R[t, h, s_kind].astype(f32) + R[t, h, d_kind].astype(f32)
                ).astype(bf)
        for h in halves:
            for kind, d, row in ((0, 2, 0), (1, 2, 96), (4, 1, 96), (5, -1, 0)):
                cp = qmove(t, h, kind, Q.at[t, h, bmod(h, d), pl.ds(row, 96)])
                cp.start()
                sent.append(cp)

    def sum4(t):
        for h in halves:
            for kind, d, row in ((2, 1, 0), (3, -1, 96)):
                qmove(t, h, kind - 2, T2.at[t, h, 0]).wait_recv()
                T2[t, h, kind - 2] = (
                    Q[t, h, bmod(h, d), pl.ds(row, 96)].astype(f32)
                    + R2[t, h, kind - 2].astype(f32)
                ).astype(bf)
                cp = qmove(t, h, kind, T2.at[t, h, kind - 2])
                cp.start()
                sent.append(cp)

    def sum5(t):
        for h in halves:
            for row, s_kind, d_kind in ((0, 2, 5), (96, 3, 4)):
                qmove(t, h, s_kind, T2.at[t, h, 0]).wait_recv()
                qmove(t, h, d_kind, T2.at[t, h, 0]).wait_recv()
                rows = (
                    S[t, h, me, pl.ds(row, 96)].astype(f32)
                    + Q[t, h, b_own[h], pl.ds(row, 96)].astype(f32)
                    + R2[t, h, s_kind].astype(f32)
                    + R2[t, h, d_kind].astype(f32)
                ).astype(bf)
                for n in range(4):
                    F[8 * t + 4 * h + n, pl.ds(row, 96)] = rows[:, 64 * n : 64 * n + 64]

    gather0(0)
    acc[...] = jnp.zeros_like(acc)
    ss[...] = jnp.zeros_like(ss)
    gather1(0)
    gather0(1)
    for c in w_in:
        c.wait()

    @pl.loop(0, 4)
    def _(g):
        gains = jnp.concatenate([gain_ref[4 * g + n] for n in range(4)], axis=1).astype(bf)
        W[g] = W[g] * gains

    @pl.loop(0, 16)
    def _(i):
        slot = jnp.int32(0)
        for j in range(16):
            slot = jnp.where(dealt_ref[0, j] == i, j, slot)
        inverse[i] = slot

    gather2(0)
    fold_a(0, z)
    gather3(0)
    gather1(1)
    gather4(0)
    fold_a(0, (z + 3) % 4)
    fold_a(0, (z + 1) % 4)
    fold_b(0, x // 2)
    gather2(1)
    gather5(0)
    fold_a(0, (z + 2) % 4)
    fold_b(0, 1 - x // 2)
    gather3(1)
    activate(0)
    gather4(1)
    dn_in.wait()
    sum1(0)
    fold_a(1, z)
    fold_a(1, (z + 3) % 4)
    fold_a(1, (z + 1) % 4)
    fold_b(1, x // 2)
    sum2(0)
    gather5(1)
    fold_a(1, (z + 2) % 4)
    fold_b(1, 1 - x // 2)
    activate(1)
    sum1(1)
    sum3(0)
    sum2(1)
    sum4(0)
    sum3(1)
    sum5(0)
    sum4(1)
    sum5(1)

    @pl.loop(0, 8)
    def _(m):
        out_ref[:, pl.ds(pl.multiple_of(m * 128, 128), 128)] = jnp.concatenate(
            [F[inverse[2 * m]], F[inverse[2 * m + 1]]], axis=1
        )

    for cp in sent:
        cp.wait_send()


def mlp_call(dealing, stream_t, weights, down_t, gain):
    anyspace = pl.BlockSpec(memory_space=pl.ANY)
    vmem = pl.BlockSpec(memory_space=pltpu.VMEM)
    bf, f32 = jnp.bfloat16, jnp.float32
    dma = pltpu.SemaphoreType.DMA
    return pl.pallas_call(
        mlp_kernel,
        out_shape=jax.ShapeDtypeStruct((192, 1024), bf),
        in_specs=[pl.BlockSpec(memory_space=pltpu.SMEM), anyspace, anyspace, anyspace, vmem],
        out_specs=vmem,
        scratch_shapes=[
            pltpu.VMEM((2, 2, 16, 192, 256), bf),
            pltpu.VMEM((4, 1024, 768), bf),
            pltpu.VMEM((3072, 512), bf),
            pltpu.VMEM((2, 2, 1024, 256), f32),
            pltpu.VMEM((2, 2, 512, 256), bf),
            pltpu.VMEM((2, 2, 1, 256), f32),
            pltpu.VMEM((2, 2, 6, 2, 192, 256), bf),
            pltpu.VMEM((2, 2, 6, 2, 192, 256), bf),
            pltpu.VMEM((2, 2, 4, 192, 256), bf),
            pltpu.VMEM((2, 2, 2, 96, 256), bf),
            pltpu.VMEM((2, 2, 6, 96, 256), bf),
            pltpu.VMEM((16, 192, 64), bf),
            pltpu.SMEM((16,), jnp.int32),
            dma((2, 2)),
            dma((9,)),
            dma((2, 2, 20)),
            dma((2, 2, 20)),
            dma((2, 2, 6)),
            dma((2, 2, 6)),
            dma((2, 2, 6)),
            dma((2, 2, 6)),
        ],
        compiler_params=pltpu.CompilerParams(
            collective_id=0, has_side_effects=True, vmem_limit_bytes=60 * 1024 * 1024
        ),
        name="mlp",
    )(dealing, stream_t, weights, down_t, gain)


def body(
    dealing,
    residual,
    queries,
    draft_keys,
    draft_values,
    cache_keys,
    cache_values,
    cache_lengths,
    parents,
    draft_counts,
    accepted,
    out_weight,
    norm_gain,
    gate_weight,
    up_weight,
    down_weight,
):
    freq = np.power(10000.0, -(np.arange(192) % 48) * (2.0 / HEAD_DIM)).astype(np.float32)

    stream_t, new_keys, new_values, gains, gate_up, down_t = attend_call(
        dealing,
        cache_lengths,
        draft_counts,
        parents,
        accepted,
        jnp.asarray(freq).reshape(1, 192),
        norm_gain,
        queries.T,
        draft_keys.T,
        draft_values.T,
        residual.T,
        out_weight.T,
        gate_weight,
        up_weight,
        down_weight,
        cache_keys,
        cache_values,
    )
    out_t = mlp_call(dealing, stream_t, gate_up, down_t.reshape(3072, 512), gains)
    return (out_t.T, new_keys, new_values)


def solution(mesh):
    placed = (
        P("row", None),
        P("row", "col"),
        P("row", "col"),
        P("row", "col"),
        P("row", "col"),
        P(("row", "col"), None, None),
        P(("row", "col"), None, None),
        P(("row", "col")),
        P(("row", "col"), None),
        P(("row", "col")),
        P(("row", "col"), None),
        P("row", "col"),
        P("col"),
        P("row", "col"),
        P("row", "col"),
        P("col", "row"),
    )
    return jax.shard_map(
        body,
        mesh=mesh,
        in_specs=placed,
        out_specs=(P("row", "col"), P(("row", "col"), None, None), P(("row", "col"), None, None)),
        check_vma=False,
    )
```
